512 devices in a mesh: track: 64 (over z, x, core), ses: 8 (over y).
Axes of the slice: x: 4, y: 8, z: 8, core: 2. Of those that a mesh axis runs over, the one named last changes fastest.
Arguments:
- jacobians: float32 [2, 9, 8, 131072], P(None, None, None, ('track', 'ses')), may hold values from -6 to 6
- direction: float32 [6, 2097152], P(None, ('track', 'ses')), may hold values from -50 to 50
- residual: float32 [6, 2097152], P(None, ('track', 'ses')), may hold values from -50 to 50
- solution: float32 [6, 2097152], P(None, ('track', 'ses')), may hold values from -6 to 6
- cam_damping: float32 [6, 2097152], P(None, ('track', 'ses')), may hold values from 0.5 to 4
- precond: float32 [6, 6, 2097152], P(None, None, ('track', 'ses')), may hold values from -0.15 to 2, as said below
- land_damping: float32 [131072], P(('track', 'ses')), may hold values from 0.5 to 4
- obs_slot: int32 [8, 131072], P(None, ('track', 'ses')), may hold values from 0 to 8191, as said below
- obs_mask: int32 [8, 131072], P(None, ('track', 'ses')), may hold values from 0 to 1, as said below
- serve_rows: int32 [512, 8192], P(('track', 'ses')), may hold values from 0 to 4095, as said below
Outputs:
- solution_new: float32 [6, 2097152], P(None, ('track', 'ses'))
- residual_new: float32 [6, 2097152], P(None, ('track', 'ses'))
- direction_new: float32 [6, 2097152], P(None, ('track', 'ses'))
The draws below stay inside these ranges and needn't reach their ends.
Inputs may be any that keep to these rules, and one draw needn't show every extreme that they name: `obs_slot`: each slot names one keyframe that device s // 16 serves to the observing device; most slots name an owner in the observing device's own session block, the rest name owners anywhere. `serve_rows`: each row block of 16 entries lists distinct local keyframe rows of the owner. `obs_mask`: A track's live observation slots come first; every track has 2 to 8. `precond`: Symmetric, with a dominant positive diagonal.
All inputs are finite; a program needn't handle non-finite values.
Results may differ from the reference program's by a relative error of at most 0.0003.
Values sent between devices are 32-bit elements; how exact they have to be, the bound alone decides.
A program may use at most 64 MiB of HBM per device.

```python
import math
import jax
import jax.numpy as jnp

TRK_DEV = 256
KF_DEV = 4096
CAP = 16
TRACKS = 131072
KF = 2097152
N_TRACK = 64
N_SES = 8
DEVICES = 512


def rising_field(key):
    k_base, k_rough = jax.random.split(key)
    position = jnp.arange(KF, dtype=jnp.float32) / KF
    roughness = jnp.exp(jax.random.uniform(k_rough, (1, KF), minval=-1.15, maxval=1.15))
    base_draw = jax.random.truncated_normal(k_base, -4.0, 4.0, (6, KF))
    growth = jnp.exp(1.1 * position)
    return (base_draw * growth[None] * roughness).astype(jnp.float32)


def draw_direction(key, part):
    return rising_field(jax.random.fold_in(key, 11))


def draw_residual(key, part):
    return rising_field(jax.random.fold_in(key, 23))


def draw_precond(key, part):
    k_off, k_diag = jax.random.split(jax.random.fold_in(key, 37))
    raw_off = jax.random.uniform(k_off, (6, 6, KF), minval=-0.075, maxval=0.075)
    symmetric = raw_off + jnp.swapaxes(raw_off, 0, 1)
    identity_mat = (jnp.arange(6)[:, None] == jnp.arange(6)[None, :]).astype(jnp.float32)[:, :, None]
    diagonal = jnp.exp(jax.random.uniform(k_diag, (6, KF), minval=0.0, maxval=0.693))
    return (symmetric * (1.0 - identity_mat) + identity_mat * diagonal[None]).astype(jnp.float32)


def draw_obs_mask(key, part):
    lengths = jax.random.randint(jax.random.fold_in(key, 41), (1, TRACKS), 2, 9)
    return (jnp.arange(8, dtype=jnp.int32)[:, None] < lengths).astype(jnp.int32)


def draw_obs_slot(key, part):
    k_pick, k_near, k_far, k_within = jax.random.split(jax.random.fold_in(key, 61), 4)
    observer = jnp.arange(TRACKS, dtype=jnp.int32)[None, :] // TRK_DEV
    own_session = observer % N_SES
    near_owner = jax.random.randint(k_near, (8, TRACKS), 0, N_TRACK) * N_SES + own_session
    far_owner = jax.random.randint(k_far, (8, TRACKS), 0, DEVICES)
    pick = jax.random.randint(k_pick, (8, TRACKS), 0, 100)
    owner = jnp.where(pick < 85, near_owner, far_owner)
    slots = owner * CAP + jax.random.randint(k_within, (8, TRACKS), 0, CAP)
    flat = jnp.arange(8 * TRACKS, dtype=jnp.int32).reshape(8, TRACKS)
    slots = jnp.where(flat == 0, 0, slots)
    slots = jnp.where(flat == 8 * TRACKS - 1, DEVICES * CAP - 1, slots)
    return slots.astype(jnp.int32)


def draw_serve_rows(key, part):
    k_off, k_start = jax.random.split(jax.random.fold_in(key, 53))
    stride = KF_DEV // CAP
    offsets = jax.random.randint(k_off, (DEVICES, DEVICES, CAP), 0, stride)
    start_row = jax.random.randint(k_start, (DEVICES, DEVICES, 1), 0, KF_DEV)
    row_ids = (jnp.arange(CAP, dtype=jnp.int32)[None, None, :] * stride + offsets + start_row) % KF_DEV
    return row_ids.reshape(DEVICES, DEVICES * CAP).astype(jnp.int32)


def shard_levels(key, shape, pieces, least, high):
    def one(dim, parts):
        draws = jax.random.uniform(jax.random.fold_in(jax.random.fold_in(key, 6), dim), (parts,), jnp.float32, least / len(pieces), high / len(pieces))
        return jnp.repeat(jnp.exp(draws), shape[dim] // parts).reshape((-1,) + (1,) * (len(shape) - dim - 1))

    loudness = one(*pieces[0])
    for cut in pieces[1:]:
        loudness = loudness * one(*cut)
    return loudness


def normal_values(key, shape, deviation, bound, pieces=(), kind=jnp.bfloat16):
    factor_of = shard_levels(key, shape, pieces, -0.22, 0.18) if pieces else 1.0
    array = jax.random.normal(key, shape, jnp.float32) * deviation * factor_of
    return jnp.minimum(jnp.maximum(array, -bound), bound).astype(kind)


def setup_inputs(seed: int = 0) -> dict:
    key_of = jax.random.split(jax.random.key(seed), 11)
    return {
        "jacobians": normal_values(key_of[0], (2, 9, 8, TRACKS), 1.0, 6.0, ((3, 512),), jnp.float32),
        "direction": draw_direction(jax.random.fold_in(key_of[10], 71), 0),
        "residual": draw_residual(jax.random.fold_in(key_of[10], 71), 0),
        "solution": normal_values(key_of[3], (6, KF), 1.0, 6.0, ((1, 512),), jnp.float32),
        "cam_damping": jnp.clip(jnp.exp(math.log(4.0) - 2.0794415 * jax.random.uniform(key_of[4], (6, KF), jnp.float32) ** shard_levels(key_of[4], (6, KF), ((1, 512),), -0.2, 0.2)), 0.5, 4.0),
        "precond": draw_precond(jax.random.fold_in(key_of[10], 71), 0),
        "land_damping": jnp.clip(jnp.exp(math.log(4.0) - 2.0794415 * jax.random.uniform(key_of[6], (TRACKS,), jnp.float32) ** shard_levels(key_of[6], (TRACKS,), ((0, 512),), -0.2, 0.2)), 0.5, 4.0),
        "obs_slot": draw_obs_slot(jax.random.fold_in(key_of[10], 71), 0),
        "obs_mask": draw_obs_mask(jax.random.fold_in(key_of[10], 71), 0),
        "serve_rows": draw_serve_rows(jax.random.fold_in(key_of[10], 71), 0),
    }


def invert_three(matrix):
    cofactor = [[matrix[(i + 1) % 3, (j + 1) % 3] * matrix[(i + 2) % 3, (j + 2) % 3]
                 - matrix[(i + 1) % 3, (j + 2) % 3] * matrix[(i + 2) % 3, (j + 1) % 3]
                 for j in range(3)] for i in range(3)]
    determinant = matrix[0, 0] * cofactor[0][0] + matrix[0, 1] * cofactor[0][1] + matrix[0, 2] * cofactor[0][2]
    adjugate = jnp.stack([jnp.stack([cofactor[j][i] for j in range(3)]) for i in range(3)])
    return adjugate / determinant[None, None]


def track_terms(jacobian, camera_rows, live_mask, land_damp):
    cam_jac = jacobian[:, 0:6]
    land_jac = jacobian[:, 6:9]
    projected = jnp.sum(cam_jac * camera_rows[None], axis=1)
    weighted = land_jac * live_mask[None, None]
    normal_mat = jnp.sum(weighted[:, :, None] * land_jac[:, None, :], axis=(0, 3))
    identity_mat = (jnp.arange(3)[:, None] == jnp.arange(3)[None, :]).astype(jnp.float32)
    normal_mat = normal_mat + identity_mat[:, :, None] * land_damp[None, None]
    inverse = invert_three(normal_mat)
    landmark_rhs = jnp.sum(weighted * projected[:, None], axis=(0, 2))
    landmark_step = jnp.sum(inverse * landmark_rhs[None], axis=1)
    back_proj = jnp.sum(land_jac * landmark_step[None, :, None], axis=1)
    obs_res = live_mask[None] * (projected - back_proj)
    return jnp.sum(cam_jac * obs_res[:, None], axis=0)


def apply_precond(precond, vector):
    return jnp.sum(precond * vector[None], axis=1)


def reference(jacobians, direction, residual, solution, cam_damping, precond, land_damping, obs_slot, obs_mask, serve_rows):
    device_index = (jnp.arange(TRACKS, dtype=jnp.int32) // TRK_DEV)[None, :]
    source = obs_slot // CAP
    within = obs_slot % CAP
    local_row = serve_rows[source, device_index * CAP + within]
    keyframe = (source * KF_DEV + local_row).astype(jnp.int32)
    camera_rows = direction[:, keyframe]
    live_mask = obs_mask.astype(jnp.float32)
    gradient = track_terms(jacobians, camera_rows, live_mask, land_damping)
    summed = jnp.zeros((6, KF), jnp.float32).at[:, keyframe.reshape(-1)].add(gradient.reshape(6, -1))
    schur_image = cam_damping * direction + summed
    old_norm = jnp.sum(residual * apply_precond(precond, residual))
    curvature = jnp.sum(direction * schur_image)
    step_size = old_norm / curvature
    solution_new = solution + step_size * direction
    residual_new = residual - step_size * schur_image
    precond_res = apply_precond(precond, residual_new)
    new_norm = jnp.sum(residual_new * precond_res)
    direction_new = precond_res + (new_norm / old_norm) * direction
    return solution_new, residual_new, direction_new
```

```python
import functools

import jax
import jax.numpy as jnp
from jax import lax
from jax.experimental import pallas as pl
from jax.experimental.pallas import tpu as pltpu
from jax.sharding import PartitionSpec as P

MESH = pl.DeviceIdType.MESH
VMEM = pl.BlockSpec(memory_space=pltpu.VMEM)
LANES = 256
SLOT = 8


def pieces(x):
    high = x.astype(jnp.bfloat16)
    low = (x - high.astype(jnp.float32)).astype(jnp.bfloat16)
    return jnp.concatenate([high, low], axis=0)


def join(x):
    half = x.shape[0] // 2
    return x[:half] + x[half:]


def one_hot(index, size):
    rows = lax.broadcasted_iota(jnp.int32, (size, index.shape[1]), 0)
    return jnp.where(rows == index, 1.0, 0.0).astype(jnp.bfloat16)


def pick(values, group):
    total = jnp.zeros((SLOT, values.shape[1]), jnp.float32)
    for g in range(values.shape[0] // SLOT):
        total += jnp.where(group == g, values[g * SLOT : (g + 1) * SLOT], 0.0)
    return total


def spread(values, group, groups):
    return jnp.concatenate([jnp.where(group == g, values, 0.0) for g in range(groups)], axis=0)


def dot(a, b):
    return lax.dot_general(a, b, (((1,), (0,)), ((), ())), preferred_element_type=jnp.float32)


def dot_nt(a, b):
    return lax.dot_general(a, b, (((1,), (1,)), ((), ())), preferred_element_type=jnp.float32)


def serve_kernel(direction_ref, rows_ref, out_ref, gathered):
    groups = direction_ref.shape[1] // LANES
    pad = jnp.zeros((2, LANES), jnp.float32)
    table = []
    for g in range(groups):
        table += [direction_ref[:, g * LANES : (g + 1) * LANES], pad]
    table = pieces(jnp.concatenate(table, axis=0))
    for w in range(rows_ref.shape[0]):
        index = rows_ref[w : w + 1, :]
        found = join(dot(table, one_hot(index & (LANES - 1), LANES)))
        gathered[w * SLOT : (w + 1) * SLOT, :] = pick(found, index // LANES)
    out_ref[...] = gathered[...].T


def inverse_times(m, rhs):
    a, b, c, d, e, f = m
    c00 = d * f - e * e
    c01 = e * c - b * f
    c02 = b * e - d * c
    c11 = f * a - c * c
    c12 = c * b - e * a
    c22 = a * d - b * b
    scale = 1.0 / (a * c00 + b * c01 + c * c02)
    x, y, z = rhs
    return (
        (c00 * x + c01 * y + c02 * z) * scale,
        (c01 * x + c11 * y + c12 * z) * scale,
        (c02 * x + c12 * y + c22 * z) * scale,
    )


def track_kernel(incoming_ref, jac_ref, damp_ref, slot_ref, mask_ref, out_ref, swap):
    devices = incoming_ref.shape[0]
    capacity = incoming_ref.shape[1] // SLOT
    slots, tracks = slot_ref.shape
    table = pieces(incoming_ref[...].T)
    for o in range(slots):
        slot = slot_ref[o : o + 1, :]
        found = join(dot(table, one_hot(slot // capacity, devices)))
        swap[o * SLOT : (o + 1) * SLOT, :] = pick(found, slot % capacity)
    rows = swap[...].reshape(slots, SLOT, tracks)
    camera = [rows[:, k, :] for k in range(6)]
    live = mask_ref[...].astype(jnp.float32)
    cam = [[jac_ref[a, k] for k in range(6)] for a in range(2)]
    land = [[jac_ref[a, 6 + i] for i in range(3)] for a in range(2)]
    projected = [sum(cam[a][k] * camera[k] for k in range(6)) for a in range(2)]
    weighted = [[land[a][i] * live for i in range(3)] for a in range(2)]

    def over(x):
        return jnp.sum(x, axis=0, keepdims=True)

    damp = damp_ref[...]
    normal = []
    for i in range(3):
        for j in range(i, 3):
            entry = over(sum(weighted[a][i] * land[a][j] for a in range(2)))
            normal.append(entry + damp if i == j else entry)
    rhs = [over(sum(weighted[a][i] * projected[a] for a in range(2))) for i in range(3)]
    step = inverse_times(normal, rhs)
    res = [live * (projected[a] - sum(land[a][i] * step[i] for i in range(3))) for a in range(2)]
    gradient = [sum(cam[a][k] * res[a] for a in range(2)) for k in range(6)]
    gradient += [jnp.zeros_like(live)] * 2
    rows = jnp.stack(gradient, axis=1)
    total = jnp.zeros((2 * capacity * SLOT, devices), jnp.float32)
    for o in range(slots):
        slot = slot_ref[o : o + 1, :]
        terms = pieces(spread(rows[o], slot % capacity, capacity))
        total += dot_nt(terms, one_hot(slot // capacity, devices))
    out_ref[...] = join(total).T


def apply_precond(precond, vector):
    total = precond[0] * vector[0:1]
    for k in range(1, 6):
        total += precond[k] * vector[k : k + 1]
    return total


def schur_kernel(
    arrived_ref, rows_ref, direction_ref, residual_ref, damp_ref, precond_ref,
    schur_ref, pre_res_ref, pre_schur_ref, sums_ref, turned,
):
    groups = direction_ref.shape[1] // LANES
    turned[...] = arrived_ref[...].T
    total = jnp.zeros((2 * groups * SLOT, LANES), jnp.float32)
    for w in range(rows_ref.shape[0]):
        index = rows_ref[w : w + 1, :]
        terms = pieces(spread(turned[w * SLOT : (w + 1) * SLOT, :], index // LANES, groups))
        total += dot_nt(terms, one_hot(index & (LANES - 1), LANES))
    total = join(total)
    sums = [jnp.zeros((6, LANES), jnp.float32) for _ in range(4)]
    for g in range(groups):
        part = pl.ds(g * LANES, LANES)
        direction = direction_ref[:, part]
        residual = residual_ref[:, part]
        precond = precond_ref[:, :, part]
        schur = damp_ref[:, part] * direction + total[g * SLOT : g * SLOT + 6]
        pre_res = apply_precond(precond, residual)
        pre_schur = apply_precond(precond, schur)
        schur_ref[:, part] = schur
        pre_res_ref[:, part] = pre_res
        pre_schur_ref[:, part] = pre_schur
        sums[0] += residual * pre_res
        sums[1] += direction * schur
        sums[2] += schur * pre_res
        sums[3] += schur * pre_schur
    lane = lax.broadcasted_iota(jnp.int32, (1, 128), 1)
    row = jnp.zeros((1, 128), jnp.float32)
    for q in range(4):
        row += jnp.where(lane == q, jnp.sum(sums[q], keepdims=True), 0.0)
    sums_ref[...] = row


def update_kernel(
    sums_ref, direction_ref, residual_ref, solution_ref, schur_ref, pre_res_ref, pre_schur_ref,
    solution_new_ref, residual_new_ref, direction_new_ref,
):
    old_norm, curvature, cross, square = [sums_ref[0:1, q : q + 1] for q in range(4)]
    step = old_norm / curvature
    ratio = (old_norm - 2.0 * step * cross + step * step * square) / old_norm
    direction = direction_ref[...]
    solution_new_ref[...] = solution_ref[...] + step * direction
    residual_new_ref[...] = residual_ref[...] - step * schur_ref[...]
    direction_new_ref[...] = pre_res_ref[...] - step * pre_schur_ref[...] + ratio * direction


def greet(tracks, sessions):
    me, ses = lax.axis_index("track"), lax.axis_index("ses")
    barrier = pltpu.get_barrier_semaphore()

    def track(i, _):
        pl.semaphore_signal(barrier, inc=1, device_id={"track": lax.rem(me + i, tracks)}, device_id_type=MESH)
        return 0

    lax.fori_loop(1, tracks, track, 0)
    for i in range(1, sessions):
        pl.semaphore_signal(barrier, inc=1, device_id={"ses": lax.rem(ses + i, sessions)}, device_id_type=MESH)
    pl.semaphore_wait(barrier, tracks + sessions - 2)
    return me, ses


def exchange_kernel(tracks, sessions, src, out, middle, send, recv, send2, recv2, local):
    me, ses = greet(tracks, sessions)

    def track(i, _):
        to = lax.rem(me + i, tracks)
        pltpu.make_async_remote_copy(
            src.at[to], middle.at[me], send, recv, device_id={"track": to}, device_id_type=MESH
        ).start()
        return 0

    lax.fori_loop(1, tracks, track, 0)
    own = pltpu.make_async_copy(src.at[me], middle.at[me], local.at[0])
    own.start()
    own.wait()
    others = pl.ds(0, tracks - 1)
    pltpu.make_async_copy(middle.at[others], middle.at[others], recv).wait()
    for i in range(1, sessions):
        to = lax.rem(ses + i, sessions)
        pltpu.make_async_remote_copy(
            middle.at[:, to], out.at[:, ses], send2.at[i], recv2.at[i], device_id={"ses": to}, device_id_type=MESH
        ).start()
    own = pltpu.make_async_copy(middle.at[:, ses], out.at[:, ses], local.at[1])
    own.start()
    own.wait()
    for i in range(1, sessions):
        block = out.at[:, lax.rem(ses - i + sessions, sessions)]
        pltpu.make_async_copy(block, block, recv2.at[i]).wait()
        block = middle.at[:, lax.rem(ses + i, sessions)]
        pltpu.make_async_copy(block, block, send2.at[i]).wait()
    pltpu.make_async_copy(src.at[others], src.at[others], send).wait()


def reduce_kernel(tracks, sessions, src, out, middle, final, partial, send, recv, send2, recv2, local):
    me, ses = greet(tracks, sessions)

    def track(i, _):
        to = lax.rem(me + i, tracks)
        pltpu.make_async_remote_copy(
            src, middle.at[me], send, recv, device_id={"track": to}, device_id_type=MESH
        ).start()
        return 0

    lax.fori_loop(1, tracks, track, 0)
    own = pltpu.make_async_copy(src, middle.at[me], local.at[0])
    own.start()
    own.wait()
    others = pl.ds(0, tracks - 1)
    pltpu.make_async_copy(middle.at[others], middle.at[others], recv).wait()
    partial[...] = jnp.sum(middle[...], axis=0)
    for i in range(1, sessions):
        to = lax.rem(ses + i, sessions)
        pltpu.make_async_remote_copy(
            partial, final.at[ses], send2.at[i], recv2.at[i], device_id={"ses": to}, device_id_type=MESH
        ).start()
    own = pltpu.make_async_copy(partial, final.at[ses], local.at[1])
    own.start()
    own.wait()
    for i in range(1, sessions):
        block = final.at[lax.rem(ses - i + sessions, sessions)]
        pltpu.make_async_copy(block, block, recv2.at[i]).wait()
        pltpu.make_async_copy(partial, partial, send2.at[i]).wait()
    out[...] = jnp.sum(final[...], axis=0)
    pltpu.make_async_copy(middle.at[others], middle.at[others], send).wait()


def semaphores(sessions):
    dma = pltpu.SemaphoreType.DMA
    return [dma, dma, dma((sessions,)), dma((sessions,)), dma((2,))]


def exchange(block, tracks, sessions, ident):
    shape = (tracks, sessions, 1, block.shape[-1])
    return pl.pallas_call(
        functools.partial(exchange_kernel, tracks, sessions),
        out_shape=jax.ShapeDtypeStruct(shape, jnp.float32),
        in_specs=[VMEM],
        out_specs=VMEM,
        scratch_shapes=[pltpu.VMEM(shape, jnp.float32)] + semaphores(sessions),
        compiler_params=pltpu.CompilerParams(collective_id=ident, has_side_effects=True),
        name="exchange",
    )(block.reshape(shape)).reshape(block.shape)


def reduce_all(row, tracks, sessions, ident):
    return pl.pallas_call(
        functools.partial(reduce_kernel, tracks, sessions),
        out_shape=jax.ShapeDtypeStruct(row.shape, jnp.float32),
        in_specs=[VMEM],
        out_specs=VMEM,
        scratch_shapes=[
            pltpu.VMEM((tracks,) + row.shape, jnp.float32),
            pltpu.VMEM((sessions,) + row.shape, jnp.float32),
            pltpu.VMEM(row.shape, jnp.float32),
        ]
        + semaphores(sessions),
        compiler_params=pltpu.CompilerParams(collective_id=ident, has_side_effects=True),
        name="reduce_all",
    )(row)


def local_call(kernel, outs, scratch, *args):
    return pl.pallas_call(
        kernel,
        out_shape=[jax.ShapeDtypeStruct(s, jnp.float32) for s in outs],
        in_specs=[VMEM] * len(args),
        out_specs=[VMEM] * len(outs),
        scratch_shapes=[pltpu.VMEM(s, jnp.float32) for s in scratch],
        name=kernel.__name__,
    )(*args)


def on_device(
    jacobians, direction, residual, solution, cam_damping, precond, land_damping, obs_slot, obs_mask, serve_rows
):
    tracks, sessions = lax.axis_size("track"), lax.axis_size("ses")
    devices = tracks * sessions
    capacity = serve_rows.size // devices
    rows = serve_rows.reshape(devices, capacity).T
    width = capacity * SLOT
    (outgoing,) = local_call(serve_kernel, [(devices, width)], [(width, devices)], direction, rows)
    incoming = exchange(outgoing, tracks, sessions, 0)
    (slot_sums,) = local_call(
        track_kernel,
        [(devices, width)],
        [(obs_slot.shape[0] * SLOT, obs_slot.shape[1])],
        incoming, jacobians, land_damping[None], obs_slot, obs_mask,
    )
    arrived = exchange(slot_sums, tracks, sessions, 1)
    shape = direction.shape
    schur, pre_res, pre_schur, sums = local_call(
        schur_kernel,
        [shape, shape, shape, (1, 128)],
        [(width, devices)],
        arrived, rows, direction, residual, cam_damping, precond,
    )
    sums = reduce_all(sums, tracks, sessions, 2)
    return tuple(
        local_call(update_kernel, [shape] * 3, [], sums, direction, residual, solution, schur, pre_res, pre_schur)
    )


def solution(mesh):
    split = ("track", "ses")
    return jax.shard_map(
        on_device,
        mesh=mesh,
        in_specs=(
            P(None, None, None, split),
            P(None, split),
            P(None, split),
            P(None, split),
            P(None, split),
            P(None, None, split),
            P(split),
            P(None, split),
            P(None, split),
            P(split, None),
        ),
        out_specs=(P(None, split), P(None, split), P(None, split)),
        check_vma=False,
    )
```

```python
import functools

import jax
import jax.numpy as jnp
from jax import lax
from jax.experimental import pallas as pl
from jax.experimental.pallas import tpu as pltpu
from jax.sharding import PartitionSpec as P

MESH = pl.DeviceIdType.MESH
VMEM = pl.BlockSpec(memory_space=pltpu.VMEM)
LANES = 256
SLOT = 8


def pieces(x):
    high = x.astype(jnp.bfloat16)
    low = (x - high.astype(jnp.float32)).astype(jnp.bfloat16)
    return jnp.concatenate([high, low], axis=0)


def join(x):
    half = x.shape[0] // 2
    return x[:half] + x[half:]


def one_hot(index, size):
    rows = lax.broadcasted_iota(jnp.int32, (size, index.shape[1]), 0)
    return jnp.where(rows == index, 1.0, 0.0).astype(jnp.bfloat16)


def pick(values, group):
    total = jnp.zeros((SLOT, values.shape[1]), jnp.float32)
    for g in range(values.shape[0] // SLOT):
        total += jnp.where(group == g, values[g * SLOT : (g + 1) * SLOT], 0.0)
    return total


def spread(values, group, groups):
    return jnp.concatenate([jnp.where(group == g, values, 0.0) for g in range(groups)], axis=0)


def dot(a, b):
    return lax.dot_general(a, b, (((1,), (0,)), ((), ())), preferred_element_type=jnp.float32)


def dot_nt(a, b):
    return lax.dot_general(a, b, (((1,), (1,)), ((), ())), preferred_element_type=jnp.float32)


def turn_rows(rows_ref, tracks, sessions, capacity, index):
    width = sessions * capacity
    turned = jnp.concatenate([rows_ref[:, t * width : (t + 1) * width] for t in range(tracks)], axis=0).T
    for w in range(capacity):
        lines = [turned[y * capacity + w : y * capacity + w + 1, :] for y in range(sessions)]
        index[w : w + 1, :] = jnp.concatenate(lines, axis=1)


def serve(direction_ref, index_ref, out_ref, gathered):
    groups = direction_ref.shape[1] // LANES
    pad = jnp.zeros((2, LANES), jnp.float32)
    table = []
    for g in range(groups):
        table += [direction_ref[:, g * LANES : (g + 1) * LANES], pad]
    table = pieces(jnp.concatenate(table, axis=0))
    for w in range(index_ref.shape[0]):
        index = index_ref[w : w + 1, :]
        found = join(dot(table, one_hot(index & (LANES - 1), LANES)))
        gathered[w * SLOT : (w + 1) * SLOT, :] = pick(found, index // LANES)
    out_ref[...] = gathered[...].T.reshape(out_ref.shape)


def inverse_times(m, rhs):
    a, b, c, d, e, f = m
    c00 = d * f - e * e
    c01 = e * c - b * f
    c02 = b * e - d * c
    c11 = f * a - c * c
    c12 = c * b - e * a
    c22 = a * d - b * b
    scale = 1.0 / (a * c00 + b * c01 + c * c02)
    x, y, z = rhs
    return (
        (c00 * x + c01 * y + c02 * z) * scale,
        (c01 * x + c11 * y + c12 * z) * scale,
        (c02 * x + c12 * y + c22 * z) * scale,
    )


def track_terms(incoming_ref, jac_ref, damp_ref, slot_ref, mask_ref, out_ref, swap):
    sessions, track_count, width = incoming_ref.shape
    devices = sessions * track_count
    capacity = width // SLOT
    slots, tracks = slot_ref.shape

    def place(o):
        slot = slot_ref[o : o + 1, :]
        owner = slot // capacity
        return lax.rem(owner, sessions) * track_count + owner // sessions, slot % capacity

    table = pieces(incoming_ref[...].reshape(devices, width).T)
    for o in range(slots):
        owner, within = place(o)
        found = join(dot(table, one_hot(owner, devices)))
        swap[o * SLOT : (o + 1) * SLOT, :] = pick(found, within)
    rows = swap[...].reshape(slots, SLOT, tracks)
    camera = [rows[:, k, :] for k in range(6)]
    live = mask_ref[...].astype(jnp.float32)
    cam = [[jac_ref[a, k] for k in range(6)] for a in range(2)]
    land = [[jac_ref[a, 6 + i] for i in range(3)] for a in range(2)]
    projected = [sum(cam[a][k] * camera[k] for k in range(6)) for a in range(2)]
    weighted = [[land[a][i] * live for i in range(3)] for a in range(2)]

    def over(x):
        return jnp.sum(x, axis=0, keepdims=True)

    damp = damp_ref[...]
    normal = []
    for i in range(3):
        for j in range(i, 3):
            entry = over(sum(weighted[a][i] * land[a][j] for a in range(2)))
            normal.append(entry + damp if i == j else entry)
    rhs = [over(sum(weighted[a][i] * projected[a] for a in range(2))) for i in range(3)]
    step = inverse_times(normal, rhs)
    res = [live * (projected[a] - sum(land[a][i] * step[i] for i in range(3))) for a in range(2)]
    gradient = [sum(cam[a][k] * res[a] for a in range(2)) for k in range(6)]
    gradient += [jnp.zeros_like(live)] * 2
    rows = jnp.stack(gradient, axis=1)
    total = jnp.zeros((2 * capacity * SLOT, devices), jnp.float32)
    for o in range(slots):
        owner, within = place(o)
        terms = pieces(spread(rows[o], within, capacity))
        total += dot_nt(terms, one_hot(owner, devices))
    out_ref[...] = join(total).T.reshape(out_ref.shape)


def apply_precond(precond, vector):
    total = precond[0] * vector[0:1]
    for k in range(1, 6):
        total += precond[k] * vector[k : k + 1]
    return total


def residual_terms(residual_ref, precond_ref, pre_res_ref):
    total = jnp.zeros((6, LANES), jnp.float32)
    for g in range(residual_ref.shape[1] // LANES):
        part = pl.ds(g * LANES, LANES)
        residual = residual_ref[:, part]
        pre_res = apply_precond(precond_ref[:, :, part], residual)
        pre_res_ref[:, part] = pre_res
        total += residual * pre_res
    return total


def schur_terms(
    arrived_ref, index_ref, direction_ref, damp_ref, precond_ref, pre_res_ref, schur_ref, pre_schur_ref, turned
):
    groups = direction_ref.shape[1] // LANES
    sessions, tracks, width = arrived_ref.shape
    turned[...] = arrived_ref[...].reshape(sessions * tracks, width).T
    total = jnp.zeros((2 * groups * SLOT, LANES), jnp.float32)
    for w in range(index_ref.shape[0]):
        index = index_ref[w : w + 1, :]
        terms = pieces(spread(turned[w * SLOT : (w + 1) * SLOT, :], index // LANES, groups))
        total += dot_nt(terms, one_hot(index & (LANES - 1), LANES))
    total = join(total)
    sums = [jnp.zeros((6, LANES), jnp.float32) for _ in range(3)]
    for g in range(groups):
        part = pl.ds(g * LANES, LANES)
        direction = direction_ref[:, part]
        schur = damp_ref[:, part] * direction + total[g * SLOT : g * SLOT + 6]
        pre_schur = apply_precond(precond_ref[:, :, part], schur)
        schur_ref[:, part] = schur
        pre_schur_ref[:, part] = pre_schur
        sums[0] += direction * schur
        sums[1] += schur * pre_res_ref[:, part]
        sums[2] += schur * pre_schur
    return sums


def sums_row(sums):
    lane = lax.broadcasted_iota(jnp.int32, (1, 128), 1)
    row = jnp.zeros((1, 128), jnp.float32)
    for q in range(4):
        row += jnp.where(lane == q, jnp.sum(sums[q], keepdims=True), 0.0)
    return row


def update_kernel(
    sums_ref, direction_ref, residual_ref, solution_ref, schur_ref, pre_res_ref, pre_schur_ref,
    solution_new_ref, residual_new_ref, direction_new_ref,
):
    old_norm, curvature, cross, square = [sums_ref[0:1, q : q + 1] for q in range(4)]
    step = old_norm / curvature
    ratio = (old_norm - 2.0 * step * cross + step * step * square) / old_norm
    direction = direction_ref[...]
    solution_new_ref[...] = solution_ref[...] + step * direction
    residual_new_ref[...] = residual_ref[...] - step * schur_ref[...]
    direction_new_ref[...] = pre_res_ref[...] - step * pre_schur_ref[...] + ratio * direction


def greet(tracks, sessions):
    me, ses = lax.axis_index("track"), lax.axis_index("ses")
    barrier = pltpu.get_barrier_semaphore()

    def track(i, _):
        pl.semaphore_signal(barrier, inc=1, device_id={"track": lax.rem(me + i, tracks)}, device_id_type=MESH)
        return 0

    lax.fori_loop(1, tracks, track, 0)
    for i in range(1, sessions):
        pl.semaphore_signal(barrier, inc=1, device_id={"ses": lax.rem(ses + i, sessions)}, device_id_type=MESH)
    return me, ses, barrier


def send_tracks(me, tracks, half, size, src, middle, send, recv):
    part = pl.ds(half * size, size)

    def track(i, _):
        to = lax.rem(me + i, tracks)
        pltpu.make_async_remote_copy(
            src.at[part, to], middle.at[part, me], send, recv, device_id={"track": to}, device_id_type=MESH
        ).start()
        return 0

    lax.fori_loop(1, tracks, track, 0)


def exchange(me, ses, tracks, sessions, src, middle, out, send, recv, send2, recv2, local, between):
    size = sessions // 2
    mine = ses // size
    halves = (1 - mine, mine)
    for h in range(2):
        send_tracks(me, tracks, halves[h], size, src, middle, send.at[h], recv.at[h])
    own = pltpu.make_async_copy(src.at[:, me], middle.at[:, me], local.at[0])
    own.start()
    result = between()
    own.wait()
    others = pl.ds(0, tracks - 1)
    waits = middle.at[pl.ds(0, size), others]
    count = 0
    for h in range(2):
        pltpu.make_async_copy(waits, waits, recv.at[h]).wait()
        for i in range(size):
            offset = i if h == 0 else i + 1
            if h == 1 and i == size - 1:
                own = pltpu.make_async_copy(middle.at[ses], out.at[ses], local.at[1])
                own.start()
                continue
            to = halves[h] * size + lax.rem(ses + offset, size)
            pltpu.make_async_remote_copy(
                middle.at[to], out.at[ses], send2.at[count], recv2.at[count],
                device_id={"ses": to}, device_id_type=MESH,
            ).start()
            count += 1
    own.wait()
    for i in range(sessions - 1):
        pltpu.make_async_copy(out.at[0], out.at[0], recv2.at[i]).wait()
    return result


def exchange_end(tracks, sessions, src, middle, send, send2):
    sent = src.at[pl.ds(0, sessions // 2), pl.ds(0, tracks - 1)]
    for h in range(2):
        pltpu.make_async_copy(sent, sent, send.at[h]).wait()
    for i in range(sessions - 1):
        pltpu.make_async_copy(middle.at[0], middle.at[0], send2.at[i]).wait()


def reduce_all(me, ses, tracks, sessions, row, out, mine, middle, partial, final, send, recv, send2, recv2, local):
    mine[...] = row

    def track(i, _):
        to = lax.rem(me + i, tracks)
        pltpu.make_async_remote_copy(
            mine, middle.at[me], send, recv, device_id={"track": to}, device_id_type=MESH
        ).start()
        return 0

    lax.fori_loop(1, tracks, track, 0)
    own = pltpu.make_async_copy(mine, middle.at[me], local.at[0])
    own.start()
    own.wait()
    others = pl.ds(0, tracks - 1)
    pltpu.make_async_copy(middle.at[others], middle.at[others], recv).wait()
    partial[...] = jnp.sum(middle[...], axis=0)
    for i in range(1, sessions):
        to = lax.rem(ses + i, sessions)
        pltpu.make_async_remote_copy(
            partial, final.at[ses], send2.at[i], recv2.at[i], device_id={"ses": to}, device_id_type=MESH
        ).start()
    own = pltpu.make_async_copy(partial, final.at[ses], local.at[1])
    own.start()
    own.wait()
    for i in range(1, sessions):
        block = final.at[lax.rem(ses - i + sessions, sessions)]
        pltpu.make_async_copy(block, block, recv2.at[i]).wait()
        pltpu.make_async_copy(partial, partial, send2.at[i]).wait()
    out[...] = jnp.sum(final[...], axis=0)
    pltpu.make_async_copy(middle.at[others], middle.at[others], send).wait()


def step_kernel(
    tracks, sessions,
    jac_ref, direction_ref, residual_ref, damp_ref, precond_ref, land_ref, slot_ref, mask_ref, rows_ref,
    schur_ref, pre_res_ref, pre_schur_ref, sums_ref,
    index, turned, swap, src1, middle1, out1, src2, middle2, out2, row, middle3, partial, final,
    sems1, sems2, sems3,
):
    me, ses, barrier = greet(tracks, sessions)
    capacity = index.shape[0]
    turn_rows(rows_ref, tracks, sessions, capacity, index)
    serve(direction_ref, index, src1, turned)
    pl.semaphore_wait(barrier, tracks + sessions - 2)
    old = exchange(
        me, ses, tracks, sessions, src1, middle1, out1, *sems1,
        lambda: residual_terms(residual_ref, precond_ref, pre_res_ref),
    )
    track_terms(out1, jac_ref, land_ref, slot_ref, mask_ref, src2, swap)
    exchange(
        me, ses, tracks, sessions, src2, middle2, out2, *sems2,
        lambda: exchange_end(tracks, sessions, src1, middle1, sems1[0], sems1[2]),
    )
    rest = schur_terms(
        out2, index, direction_ref, damp_ref, precond_ref, pre_res_ref, schur_ref, pre_schur_ref, turned
    )
    reduce_all(
        me, ses, tracks, sessions, sums_row([old] + rest), sums_ref, row, middle3, partial, final, *sems3
    )
    exchange_end(tracks, sessions, src2, middle2, sems2[0], sems2[2])


def local_call(kernel, outs, scratch, *args):
    return pl.pallas_call(
        kernel,
        out_shape=[jax.ShapeDtypeStruct(s, jnp.float32) for s in outs],
        in_specs=[VMEM] * len(args),
        out_specs=[VMEM] * len(outs),
        scratch_shapes=[pltpu.VMEM(s, jnp.float32) for s in scratch],
        name=kernel.__name__,
    )(*args)


def on_device(
    jacobians, direction, residual, solution, cam_damping, precond, land_damping, obs_slot, obs_mask, serve_rows
):
    tracks, sessions = lax.axis_size("track"), lax.axis_size("ses")
    devices = tracks * sessions
    capacity = serve_rows.size // devices
    width = capacity * SLOT
    shape = direction.shape
    dma = pltpu.SemaphoreType.DMA
    block = pltpu.VMEM((sessions, tracks, width), jnp.float32)
    line = (1, 128)
    sems = [dma((2,)), dma((2,)), dma((sessions,)), dma((sessions,)), dma((2,))]
    args = (
        jacobians, direction, residual, cam_damping, precond, land_damping[None], obs_slot, obs_mask, serve_rows
    )
    schur, pre_res, pre_schur, sums = pl.pallas_call(
        functools.partial(step_kernel, tracks, sessions),
        out_shape=[jax.ShapeDtypeStruct(s, jnp.float32) for s in (shape, shape, shape, line)],
        in_specs=[VMEM] * len(args),
        out_specs=[VMEM] * 4,
        scratch_shapes=[
            pltpu.VMEM((capacity, devices), jnp.int32),
            pltpu.VMEM((width, devices), jnp.float32),
            pltpu.VMEM((obs_slot.shape[0] * SLOT, obs_slot.shape[1]), jnp.float32),
        ]
        + [block] * 6
        + [
            pltpu.VMEM(line, jnp.float32),
            pltpu.VMEM((tracks,) + line, jnp.float32),
            pltpu.VMEM(line, jnp.float32),
            pltpu.VMEM((sessions,) + line, jnp.float32),
            tuple(sems),
            tuple(sems),
            (dma, dma, dma((sessions,)), dma((sessions,)), dma((2,))),
        ],
        compiler_params=pltpu.CompilerParams(collective_id=0, has_side_effects=True),
        name="step",
    )(*args)
    return tuple(
        local_call(update_kernel, [shape] * 3, [], sums, direction, residual, solution, schur, pre_res, pre_schur)
    )


def solution(mesh):
    split = ("track", "ses")
    return jax.shard_map(
        on_device,
        mesh=mesh,
        in_specs=(
            P(None, None, None, split),
            P(None, split),
            P(None, split),
            P(None, split),
            P(None, split),
            P(None, None, split),
            P(split),
            P(None, split),
            P(None, split),
            P(split, None),
        ),
        out_specs=(P(None, split), P(None, split), P(None, split)),
        check_vma=False,
    )
```

```python
import functools

import jax
import jax.numpy as jnp
from jax import lax
from jax.experimental import pallas as pl
from jax.experimental.pallas import tpu as pltpu
from jax.sharding import PartitionSpec as P

MESH = pl.DeviceIdType.MESH
VMEM = pl.BlockSpec(memory_space=pltpu.VMEM)
LANES = 256
KEYS = 6
SLOT = 8


def pieces(x):
    high = x.astype(jnp.bfloat16)
    low = (x - high.astype(jnp.float32)).astype(jnp.bfloat16)
    return jnp.concatenate([high, low], axis=0)


def join(x):
    half = x.shape[0] // 2
    return x[:half] + x[half:]


def one_hot(index, size):
    rows = lax.broadcasted_iota(jnp.int32, (size, index.shape[1]), 0)
    return jnp.where(rows == index, 1.0, 0.0).astype(jnp.bfloat16)


def pick(values, group):
    total = jnp.zeros((SLOT, values.shape[1]), jnp.float32)
    for g in range(values.shape[0] // SLOT):
        total += jnp.where(group == g, values[g * SLOT : (g + 1) * SLOT], 0.0)
    return total


def spread(values, group, groups):
    return jnp.concatenate([jnp.where(group == g, values, 0.0) for g in range(groups)], axis=0)


def slot_mask(within, capacity):
    return lax.broadcasted_iota(jnp.int32, (capacity, within.shape[1]), 0) == within


def dot(a, b):
    return lax.dot_general(a, b, (((1,), (0,)), ((), ())), preferred_element_type=jnp.float32)


def dot_nt(a, b):
    return lax.dot_general(a, b, (((1,), (1,)), ((), ())), preferred_element_type=jnp.float32)


def turn_rows(rows_ref, tracks, sessions, capacity, index):
    width = sessions * capacity
    turned = jnp.concatenate([rows_ref[:, t * width : (t + 1) * width] for t in range(tracks)], axis=0).T
    for w in range(capacity):
        lines = [turned[y * capacity + w : y * capacity + w + 1, :] for y in range(sessions)]
        index[w : w + 1, :] = jnp.concatenate(lines, axis=1)


def serve(direction_ref, index_ref, hot_ref, out_ref, tiles):
    groups = direction_ref.shape[1] // LANES
    capacity = index_ref.shape[0]
    pad = jnp.zeros((2, LANES), jnp.float32)
    table = []
    for g in range(groups):
        table += [direction_ref[:, g * LANES : (g + 1) * LANES], pad]
    table = pieces(jnp.concatenate(table, axis=0))
    for w in range(capacity):
        index = index_ref[w : w + 1, :]
        hot = one_hot(index & (LANES - 1), LANES)
        hot_ref[w] = hot
        found = pick(join(dot(table, hot)), index // LANES)
        for j in range(tiles.shape[0]):
            tiles[j, pl.ds(w, SLOT, stride=capacity), :] = found[:, j * 128 : (j + 1) * 128]
    turned = [tiles[j, : KEYS * capacity, :].T for j in range(tiles.shape[0])]
    out_ref[...] = jnp.concatenate(turned, axis=0).reshape(out_ref.shape)


def inverse_times(m, rhs):
    a, b, c, d, e, f = m
    c00 = d * f - e * e
    c01 = e * c - b * f
    c02 = b * e - d * c
    c11 = f * a - c * c
    c12 = c * b - e * a
    c22 = a * d - b * b
    scale = 1.0 / (a * c00 + b * c01 + c * c02)
    x, y, z = rhs
    return (
        (c00 * x + c01 * y + c02 * z) * scale,
        (c01 * x + c11 * y + c12 * z) * scale,
        (c02 * x + c12 * y + c22 * z) * scale,
    )


def owner_hots(slot_ref, sessions, tracks, capacity, hot_ref):
    for o in range(slot_ref.shape[0]):
        owner = slot_ref[o : o + 1, :] // capacity
        place = lax.rem(owner, sessions) * tracks + owner // sessions
        hot_ref[o] = one_hot(place, sessions * tracks)


def track_terms(incoming_ref, jac_ref, damp_ref, slot_ref, mask_ref, hot_ref, out_ref, swap):
    sessions, track_count, width = incoming_ref.shape
    devices = sessions * track_count
    capacity = width // KEYS
    slots = slot_ref.shape[0]
    table = pieces(incoming_ref[...].reshape(devices, width).T)
    masks = [slot_mask(slot_ref[o : o + 1, :] % capacity, capacity) for o in range(slots)]
    for o in range(slots):
        found = join(dot(table, hot_ref[o]))
        for k in range(KEYS):
            chosen = jnp.where(masks[o], found[k * capacity : (k + 1) * capacity], 0.0)
            swap[k * slots + o : k * slots + o + 1, :] = jnp.sum(chosen, axis=0, keepdims=True)
    camera = [swap[k * slots : (k + 1) * slots, :] for k in range(KEYS)]
    live = mask_ref[...].astype(jnp.float32)
    cam = [[jac_ref[a, k] for k in range(6)] for a in range(2)]
    land = [[jac_ref[a, 6 + i] for i in range(3)] for a in range(2)]
    projected = [sum(cam[a][k] * camera[k] for k in range(6)) for a in range(2)]
    weighted = [[land[a][i] * live for i in range(3)] for a in range(2)]

    def over(x):
        return jnp.sum(x, axis=0, keepdims=True)

    damp = damp_ref[...]
    normal = []
    for i in range(3):
        for j in range(i, 3):
            entry = over(sum(weighted[a][i] * land[a][j] for a in range(2)))
            normal.append(entry + damp if i == j else entry)
    rhs = [over(sum(weighted[a][i] * projected[a] for a in range(2))) for i in range(3)]
    step = inverse_times(normal, rhs)
    res = [live * (projected[a] - sum(land[a][i] * step[i] for i in range(3))) for a in range(2)]
    gradient = [sum(cam[a][k] * res[a] for a in range(2)) for k in range(6)]
    total = jnp.zeros((2 * width, devices), jnp.float32)
    for o in range(slots):
        terms = [jnp.where(masks[o], gradient[k][o : o + 1], 0.0) for k in range(KEYS)]
        total += dot_nt(pieces(jnp.concatenate(terms, axis=0)), hot_ref[o])
    out_ref[...] = join(total).T.reshape(out_ref.shape)


def apply_precond(precond, vector):
    total = precond[0] * vector[0:1]
    for k in range(1, 6):
        total += precond[k] * vector[k : k + 1]
    return total


def residual_terms(residual_ref, precond_ref, pre_res_ref):
    total = jnp.zeros((6, LANES), jnp.float32)
    for g in range(residual_ref.shape[1] // LANES):
        part = pl.ds(g * LANES, LANES)
        residual = residual_ref[:, part]
        pre_res = apply_precond(precond_ref[:, :, part], residual)
        pre_res_ref[:, part] = pre_res
        total += residual * pre_res
    return total


def schur_terms(
    arrived_ref, index_ref, hot_ref, direction_ref, damp_ref, precond_ref, pre_res_ref, schur_ref, pre_schur_ref, tiles
):
    groups = direction_ref.shape[1] // LANES
    sessions, tracks, width = arrived_ref.shape
    capacity = index_ref.shape[0]
    turned = arrived_ref[...].reshape(sessions * tracks, width).T
    count = tiles.shape[0]
    for j in range(count):
        tiles[j, :width, :] = turned[:, j * 128 : (j + 1) * 128]
    total = jnp.zeros((2 * groups * SLOT, LANES), jnp.float32)
    for w in range(index_ref.shape[0]):
        index = index_ref[w : w + 1, :]
        lines = [tiles[j, pl.ds(w, SLOT, stride=capacity), :] for j in range(count)]
        terms = pieces(spread(jnp.concatenate(lines, axis=1), index // LANES, groups))
        total += dot_nt(terms, hot_ref[w])
    total = join(total)
    sums = [jnp.zeros((6, LANES), jnp.float32) for _ in range(3)]
    for g in range(groups):
        part = pl.ds(g * LANES, LANES)
        direction = direction_ref[:, part]
        schur = damp_ref[:, part] * direction + total[g * SLOT : g * SLOT + 6]
        pre_schur = apply_precond(precond_ref[:, :, part], schur)
        schur_ref[:, part] = schur
        pre_schur_ref[:, part] = pre_schur
        sums[0] += direction * schur
        sums[1] += schur * pre_res_ref[:, part]
        sums[2] += schur * pre_schur
    return sums


def sums_row(sums):
    lane = lax.broadcasted_iota(jnp.int32, (1, 128), 1)
    row = jnp.zeros((1, 128), jnp.float32)
    for q in range(4):
        row += jnp.where(lane == q, jnp.sum(sums[q], keepdims=True), 0.0)
    return row


def update_kernel(
    sums_ref, direction_ref, residual_ref, solution_ref, schur_ref, pre_res_ref, pre_schur_ref,
    solution_new_ref, residual_new_ref, direction_new_ref,
):
    old_norm, curvature, cross, square = [sums_ref[0:1, q : q + 1] for q in range(4)]
    step = old_norm / curvature
    ratio = (old_norm - 2.0 * step * cross + step * step * square) / old_norm
    direction = direction_ref[...]
    solution_new_ref[...] = solution_ref[...] + step * direction
    residual_new_ref[...] = residual_ref[...] - step * schur_ref[...]
    direction_new_ref[...] = pre_res_ref[...] - step * pre_schur_ref[...] + ratio * direction


def greet(tracks, sessions):
    me, ses = lax.axis_index("track"), lax.axis_index("ses")
    barrier = pltpu.get_barrier_semaphore()

    def track(i, _):
        pl.semaphore_signal(barrier, inc=1, device_id={"track": lax.rem(me + i, tracks)}, device_id_type=MESH)
        return 0

    lax.fori_loop(1, tracks, track, 0)
    for i in range(1, sessions):
        pl.semaphore_signal(barrier, inc=1, device_id={"ses": lax.rem(ses + i, sessions)}, device_id_type=MESH)
    return me, ses, barrier


def send_tracks(me, tracks, half, size, src, middle, send, recv):
    part = pl.ds(half * size, size)

    def track(i, _):
        to = lax.rem(me + i, tracks)
        pltpu.make_async_remote_copy(
            src.at[part, to], middle.at[part, me], send, recv, device_id={"track": to}, device_id_type=MESH
        ).start()
        return 0

    lax.fori_loop(1, tracks, track, 0)


def exchange(me, ses, tracks, sessions, src, middle, out, send, recv, send2, recv2, local, between):
    size = sessions // 2
    mine = ses // size
    halves = (1 - mine, mine)
    for h in range(2):
        send_tracks(me, tracks, halves[h], size, src, middle, send.at[h], recv.at[h])
    own = pltpu.make_async_copy(src.at[:, me], middle.at[:, me], local.at[0])
    own.start()
    result = between()
    own.wait()
    others = pl.ds(0, tracks - 1)
    waits = middle.at[pl.ds(0, size), others]
    count = 0
    for h in range(2):
        pltpu.make_async_copy(waits, waits, recv.at[h]).wait()
        for i in range(size):
            offset = i if h == 0 else i + 1
            if h == 1 and i == size - 1:
                own = pltpu.make_async_copy(middle.at[ses], out.at[ses], local.at[1])
                own.start()
                continue
            to = halves[h] * size + lax.rem(ses + offset, size)
            pltpu.make_async_remote_copy(
                middle.at[to], out.at[ses], send2.at[count], recv2.at[count],
                device_id={"ses": to}, device_id_type=MESH,
            ).start()
            count += 1
    own.wait()
    for i in range(sessions - 1):
        pltpu.make_async_copy(out.at[0], out.at[0], recv2.at[i]).wait()
    return result


def exchange_end(tracks, sessions, src, middle, send, send2):
    sent = src.at[pl.ds(0, sessions // 2), pl.ds(0, tracks - 1)]
    for h in range(2):
        pltpu.make_async_copy(sent, sent, send.at[h]).wait()
    for i in range(sessions - 1):
        pltpu.make_async_copy(middle.at[0], middle.at[0], send2.at[i]).wait()


def reduce_all(me, ses, tracks, sessions, row, out, mine, middle, partial, final, send, recv, send2, recv2, local):
    mine[...] = row

    def track(i, _):
        to = lax.rem(me + i, tracks)
        pltpu.make_async_remote_copy(
            mine, middle.at[me], send, recv, device_id={"track": to}, device_id_type=MESH
        ).start()
        return 0

    lax.fori_loop(1, tracks, track, 0)
    own = pltpu.make_async_copy(mine, middle.at[me], local.at[0])
    own.start()
    own.wait()
    others = pl.ds(0, tracks - 1)
    pltpu.make_async_copy(middle.at[others], middle.at[others], recv).wait()
    partial[...] = jnp.sum(middle[...], axis=0)
    for i in range(1, sessions):
        to = lax.rem(ses + i, sessions)
        pltpu.make_async_remote_copy(
            partial, final.at[ses], send2.at[i], recv2.at[i], device_id={"ses": to}, device_id_type=MESH
        ).start()
    own = pltpu.make_async_copy(partial, final.at[ses], local.at[1])
    own.start()
    own.wait()
    for i in range(1, sessions):
        block = final.at[lax.rem(ses - i + sessions, sessions)]
        pltpu.make_async_copy(block, block, recv2.at[i]).wait()
        pltpu.make_async_copy(partial, partial, send2.at[i]).wait()
    out[...] = jnp.sum(final[...], axis=0)
    pltpu.make_async_copy(middle.at[others], middle.at[others], send).wait()


def step_kernel(
    tracks, sessions,
    direction_ref, rows_ref, slot_ref, mask_ref, land_ref, jac_hbm, residual_hbm, damp_hbm, precond_hbm,
    schur_ref, pre_res_ref, pre_schur_ref, sums_ref,
    jac_ref, residual_ref, damp_ref, precond_ref, loads,
    index, tiles, swap, hot, owner_hot, src1, middle1, out1, src2, middle2, out2, row, middle3, partial, final,
    sems1, sems2, sems3,
):
    me, ses, barrier = greet(tracks, sessions)
    pairs = ((residual_hbm, residual_ref), (precond_hbm, precond_ref), (jac_hbm, jac_ref), (damp_hbm, damp_ref))
    copies = [pltpu.make_async_copy(src, dst, loads.at[i]) for i, (src, dst) in enumerate(pairs)]
    for copy in copies:
        copy.start()
    capacity = index.shape[0]
    turn_rows(rows_ref, tracks, sessions, capacity, index)
    serve(direction_ref, index, hot, src1, tiles)
    pl.semaphore_wait(barrier, tracks + sessions - 2)

    def during_first():
        for copy in copies:
            copy.wait()
        owner_hots(slot_ref, sessions, tracks, capacity, owner_hot)
        return residual_terms(residual_ref, precond_ref, pre_res_ref)

    old = exchange(me, ses, tracks, sessions, src1, middle1, out1, *sems1, during_first)
    track_terms(out1, jac_ref, land_ref, slot_ref, mask_ref, owner_hot, src2, swap)
    exchange(
        me, ses, tracks, sessions, src2, middle2, out2, *sems2,
        lambda: exchange_end(tracks, sessions, src1, middle1, sems1[0], sems1[2]),
    )
    rest = schur_terms(
        out2, index, hot, direction_ref, damp_ref, precond_ref, pre_res_ref, schur_ref, pre_schur_ref, tiles
    )
    reduce_all(
        me, ses, tracks, sessions, sums_row([old] + rest), sums_ref, row, middle3, partial, final, *sems3
    )
    exchange_end(tracks, sessions, src2, middle2, sems2[0], sems2[2])


def local_call(kernel, outs, scratch, *args):
    return pl.pallas_call(
        kernel,
        out_shape=[jax.ShapeDtypeStruct(s, jnp.float32) for s in outs],
        in_specs=[VMEM] * len(args),
        out_specs=[VMEM] * len(outs),
        scratch_shapes=[pltpu.VMEM(s, jnp.float32) for s in scratch],
        name=kernel.__name__,
    )(*args)


def on_device(
    jacobians, direction, residual, solution, cam_damping, precond, land_damping, obs_slot, obs_mask, serve_rows
):
    tracks, sessions = lax.axis_size("track"), lax.axis_size("ses")
    devices = tracks * sessions
    capacity = serve_rows.size // devices
    width = capacity * KEYS
    slots, observed = obs_slot.shape
    shape = direction.shape
    dma = pltpu.SemaphoreType.DMA
    block = pltpu.VMEM((sessions, tracks, width), jnp.float32)
    line = (1, 128)
    sems = [dma((2,)), dma((2,)), dma((sessions,)), dma((sessions,)), dma((2,))]
    small = (direction, serve_rows, obs_slot, obs_mask, land_damping[None])
    large = (jacobians, residual, cam_damping, precond)
    schur, pre_res, pre_schur, sums = pl.pallas_call(
        functools.partial(step_kernel, tracks, sessions),
        out_shape=[jax.ShapeDtypeStruct(s, jnp.float32) for s in (shape, shape, shape, line)],
        in_specs=[VMEM] * len(small) + [pl.BlockSpec(memory_space=pl.ANY)] * len(large),
        out_specs=[VMEM] * 4,
        scratch_shapes=[pltpu.VMEM(x.shape, x.dtype) for x in large]
        + [
            dma((len(large),)),
            pltpu.VMEM((capacity, devices), jnp.int32),
            pltpu.VMEM((devices // 128, capacity * SLOT, 128), jnp.float32),
            pltpu.VMEM((slots * KEYS, observed), jnp.float32),
            pltpu.VMEM((capacity, LANES, devices), jnp.bfloat16),
            pltpu.VMEM((slots, devices, observed), jnp.bfloat16),
        ]
        + [block] * 6
        + [
            pltpu.VMEM(line, jnp.float32),
            pltpu.VMEM((tracks,) + line, jnp.float32),
            pltpu.VMEM(line, jnp.float32),
            pltpu.VMEM((sessions,) + line, jnp.float32),
            tuple(sems),
            tuple(sems),
            (dma, dma, dma((sessions,)), dma((sessions,)), dma((2,))),
        ],
        compiler_params=pltpu.CompilerParams(collective_id=0, has_side_effects=True),
        name="step",
    )(*small, *large)
    return tuple(
        local_call(update_kernel, [shape] * 3, [], sums, direction, residual, solution, schur, pre_res, pre_schur)
    )


def solution(mesh):
    split = ("track", "ses")
    return jax.shard_map(
        on_device,
        mesh=mesh,
        in_specs=(
            P(None, None, None, split),
            P(None, split),
            P(None, split),
            P(None, split),
            P(None, split),
            P(None, None, split),
            P(split),
            P(None, split),
            P(None, split),
            P(split, None),
        ),
        out_specs=(P(None, split), P(None, split), P(None, split)),
        check_vma=False,
    )
```

```python
import functools

import jax
import jax.numpy as jnp
from jax import lax
from jax.experimental import pallas as pl
from jax.experimental.pallas import tpu as pltpu
from jax.sharding import PartitionSpec as P

MESH = pl.DeviceIdType.MESH
VMEM = pl.BlockSpec(memory_space=pltpu.VMEM)
LANES = 256
KEYS = 6
SLOT = 8


def pieces(x):
    high = x.astype(jnp.bfloat16)
    low = (x - high.astype(jnp.float32)).astype(jnp.bfloat16)
    return jnp.concatenate([high, low], axis=0)


def join(x):
    half = x.shape[0] // 2
    return x[:half] + x[half:]


def one_hot(index, size):
    rows = lax.broadcasted_iota(jnp.int32, (size, index.shape[1]), 0)
    return jnp.where(rows == index, 1.0, 0.0).astype(jnp.bfloat16)


def pick(values, group):
    total = jnp.zeros((SLOT, values.shape[1]), jnp.float32)
    for g in range(values.shape[0] // SLOT):
        total += jnp.where(group == g, values[g * SLOT : (g + 1) * SLOT], 0.0)
    return total


def spread(values, group, groups):
    return jnp.concatenate([jnp.where(group == g, values, 0.0) for g in range(groups)], axis=0)


def slot_mask(within, capacity):
    return lax.broadcasted_iota(jnp.int32, (capacity, within.shape[1]), 0) == within


def dot(a, b):
    return lax.dot_general(a, b, (((1,), (0,)), ((), ())), preferred_element_type=jnp.float32)


def dot_nt(a, b):
    return lax.dot_general(a, b, (((1,), (1,)), ((), ())), preferred_element_type=jnp.float32)


def turn_rows(rows_ref, tracks, sessions, capacity, index):
    width = sessions * capacity
    turned = jnp.concatenate([rows_ref[:, t * width : (t + 1) * width] for t in range(tracks)], axis=0).T
    for w in range(capacity):
        lines = [turned[y * capacity + w : y * capacity + w + 1, :] for y in range(sessions)]
        index[w : w + 1, :] = jnp.concatenate(lines, axis=1)


def serve(direction_ref, index_ref, hot_ref, out_ref, tiles):
    groups = direction_ref.shape[1] // LANES
    capacity = index_ref.shape[0]
    pad = jnp.zeros((2, LANES), jnp.float32)
    table = []
    for g in range(groups):
        table += [direction_ref[:, g * LANES : (g + 1) * LANES], pad]
    table = pieces(jnp.concatenate(table, axis=0))
    for w in range(capacity):
        index = index_ref[w : w + 1, :]
        hot = one_hot(index & (LANES - 1), LANES)
        hot_ref[w] = hot
        found = pick(join(dot(table, hot)), index // LANES)
        for j in range(tiles.shape[0]):
            tiles[j, pl.ds(w, SLOT, stride=capacity), :] = found[:, j * 128 : (j + 1) * 128]
    turned = [tiles[j, : KEYS * capacity, :].T for j in range(tiles.shape[0])]
    out_ref[...] = jnp.concatenate(turned, axis=0).reshape(out_ref.shape)


def inverse_times(m, rhs):
    a, b, c, d, e, f = m
    c00 = d * f - e * e
    c01 = e * c - b * f
    c02 = b * e - d * c
    c11 = f * a - c * c
    c12 = c * b - e * a
    c22 = a * d - b * b
    scale = 1.0 / (a * c00 + b * c01 + c * c02)
    x, y, z = rhs
    return (
        (c00 * x + c01 * y + c02 * z) * scale,
        (c01 * x + c11 * y + c12 * z) * scale,
        (c02 * x + c12 * y + c22 * z) * scale,
    )


def owner_hots(slot_ref, sessions, tracks, capacity, hot_ref):
    for o in range(slot_ref.shape[0]):
        owner = slot_ref[o : o + 1, :] // capacity
        place = lax.rem(owner, sessions) * tracks + owner // sessions
        hot_ref[o] = one_hot(place, sessions * tracks)


def track_terms(incoming_ref, jac_ref, damp_ref, slot_ref, mask_ref, hot_ref, out_ref, swap):
    sessions, track_count, width = incoming_ref.shape
    devices = sessions * track_count
    capacity = width // KEYS
    slots = slot_ref.shape[0]
    table = pieces(incoming_ref[...].reshape(devices, width).T)
    masks = [slot_mask(slot_ref[o : o + 1, :] % capacity, capacity) for o in range(slots)]
    for o in range(slots):
        found = join(dot(table, hot_ref[o]))
        for k in range(KEYS):
            chosen = jnp.where(masks[o], found[k * capacity : (k + 1) * capacity], 0.0)
            swap[k * slots + o : k * slots + o + 1, :] = jnp.sum(chosen, axis=0, keepdims=True)
    camera = [swap[k * slots : (k + 1) * slots, :] for k in range(KEYS)]
    live = mask_ref[...].astype(jnp.float32)
    cam = [[jac_ref[a, k] for k in range(6)] for a in range(2)]
    land = [[jac_ref[a, 6 + i] for i in range(3)] for a in range(2)]
    projected = [sum(cam[a][k] * camera[k] for k in range(6)) for a in range(2)]
    weighted = [[land[a][i] * live for i in range(3)] for a in range(2)]

    def over(x):
        return jnp.sum(x, axis=0, keepdims=True)

    damp = damp_ref[...]
    normal = []
    for i in range(3):
        for j in range(i, 3):
            entry = over(sum(weighted[a][i] * land[a][j] for a in range(2)))
            normal.append(entry + damp if i == j else entry)
    rhs = [over(sum(weighted[a][i] * projected[a] for a in range(2))) for i in range(3)]
    step = inverse_times(normal, rhs)
    res = [live * (projected[a] - sum(land[a][i] * step[i] for i in range(3))) for a in range(2)]
    gradient = [sum(cam[a][k] * res[a] for a in range(2)) for k in range(6)]
    total = jnp.zeros((2 * width, devices), jnp.float32)
    for o in range(slots):
        terms = [jnp.where(masks[o], gradient[k][o : o + 1], 0.0) for k in range(KEYS)]
        total += dot_nt(pieces(jnp.concatenate(terms, axis=0)), hot_ref[o])
    out_ref[...] = join(total).T.reshape(out_ref.shape)


def apply_precond(precond, vector):
    total = precond[0] * vector[0:1]
    for k in range(1, 6):
        total += precond[k] * vector[k : k + 1]
    return total


def residual_terms(residual_ref, precond_ref, pre_res_ref):
    total = jnp.zeros((6, LANES), jnp.float32)
    for g in range(residual_ref.shape[1] // LANES):
        part = pl.ds(g * LANES, LANES)
        residual = residual_ref[:, part]
        pre_res = apply_precond(precond_ref[:, :, part], residual)
        pre_res_ref[:, part] = pre_res
        total += residual * pre_res
    return total


def schur_terms(
    arrived_ref, index_ref, hot_ref, direction_ref, damp_ref, precond_ref, pre_res_ref, schur_ref, pre_schur_ref, tiles
):
    groups = direction_ref.shape[1] // LANES
    sessions, tracks, width = arrived_ref.shape
    capacity = index_ref.shape[0]
    turned = arrived_ref[...].reshape(sessions * tracks, width).T
    count = tiles.shape[0]
    for j in range(count):
        tiles[j, :width, :] = turned[:, j * 128 : (j + 1) * 128]
    total = jnp.zeros((2 * groups * SLOT, LANES), jnp.float32)
    for w in range(index_ref.shape[0]):
        index = index_ref[w : w + 1, :]
        lines = [tiles[j, pl.ds(w, SLOT, stride=capacity), :] for j in range(count)]
        terms = pieces(spread(jnp.concatenate(lines, axis=1), index // LANES, groups))
        total += dot_nt(terms, hot_ref[w])
    total = join(total)
    sums = [jnp.zeros((6, LANES), jnp.float32) for _ in range(3)]
    for g in range(groups):
        part = pl.ds(g * LANES, LANES)
        direction = direction_ref[:, part]
        schur = damp_ref[:, part] * direction + total[g * SLOT : g * SLOT + 6]
        pre_schur = apply_precond(precond_ref[:, :, part], schur)
        schur_ref[:, part] = schur
        pre_schur_ref[:, part] = pre_schur
        sums[0] += direction * schur
        sums[1] += schur * pre_res_ref[:, part]
        sums[2] += schur * pre_schur
    return sums


def sums_row(sums):
    lane = lax.broadcasted_iota(jnp.int32, (1, 128), 1)
    row = jnp.zeros((1, 128), jnp.float32)
    for q in range(4):
        row += jnp.where(lane == q, jnp.sum(sums[q], keepdims=True), 0.0)
    return row


def update_kernel(
    sums_ref, direction_ref, residual_ref, solution_ref, schur_ref, pre_res_ref, pre_schur_ref,
    solution_new_ref, residual_new_ref, direction_new_ref,
):
    old_norm, curvature, cross, square = [sums_ref[0:1, q : q + 1] for q in range(4)]
    step = old_norm / curvature
    ratio = (old_norm - 2.0 * step * cross + step * step * square) / old_norm
    direction = direction_ref[...]
    solution_new_ref[...] = solution_ref[...] + step * direction
    residual_new_ref[...] = residual_ref[...] - step * schur_ref[...]
    direction_new_ref[...] = pre_res_ref[...] - step * pre_schur_ref[...] + ratio * direction


def greet(tracks, sessions):
    me, ses = lax.axis_index("track"), lax.axis_index("ses")
    barrier = pltpu.get_barrier_semaphore()

    def track(i, _):
        pl.semaphore_signal(barrier, inc=1, device_id={"track": lax.rem(me + i, tracks)}, device_id_type=MESH)
        return 0

    lax.fori_loop(1, tracks, track, 0)
    for i in range(1, sessions):
        pl.semaphore_signal(barrier, inc=1, device_id={"ses": lax.rem(ses + i, sessions)}, device_id_type=MESH)
    return me, ses, barrier


def send_tracks(me, tracks, src, src_at, size, dst, dst_at, send, recv):
    def track(i, _):
        to = lax.rem(me + i, tracks)
        pltpu.make_async_remote_copy(
            src.at[pl.ds(src_at, size), to], dst.at[pl.ds(dst_at, size), me], send, recv,
            device_id={"track": to}, device_id_type=MESH,
        ).start()
        return 0

    lax.fori_loop(1, tracks, track, 0)


def send_session(ses, to, src, dst, send, recv):
    pltpu.make_async_remote_copy(src, dst, send, recv, device_id={"ses": to}, device_id_type=MESH).start()


def exchange(me, ses, tracks, sessions, src, middle, out, send, recv, send2, recv2, local, between):
    size = sessions // 2
    mine = ses // size * size
    other = size - mine
    inner = lax.rem(ses, size)
    for i in range(1, size):
        to = mine + lax.rem(inner + i, size)
        send_session(ses, to, src.at[to], middle.at[ses], send2.at[i], recv2.at[i])
    send_tracks(me, tracks, src, other, size, middle, other, send.at[0], recv.at[0])
    own = [
        pltpu.make_async_copy(src.at[ses], middle.at[ses], local.at[0]),
        pltpu.make_async_copy(src.at[pl.ds(other, size), me], middle.at[pl.ds(other, size), me], local.at[1]),
    ]
    for copy in own:
        copy.start()
    for copy in own:
        copy.wait()
    for i in range(1, size):
        pltpu.make_async_copy(out.at[0], out.at[0], recv2.at[i]).wait()
    send_tracks(me, tracks, middle, mine, size, out, mine, send.at[1], recv.at[1])
    result = between()
    waits = out.at[pl.ds(0, size), pl.ds(0, tracks - 1)]
    pltpu.make_async_copy(waits, waits, recv.at[0]).wait()
    for i in range(size):
        to = other + lax.rem(inner + i, size)
        send_session(ses, to, middle.at[to], out.at[ses], send2.at[size + i], recv2.at[size + i])
    last = pltpu.make_async_copy(middle.at[pl.ds(mine, size), me], out.at[pl.ds(mine, size), me], local.at[0])
    last.start()
    last.wait()
    pltpu.make_async_copy(waits, waits, recv.at[1]).wait()
    for i in range(size):
        pltpu.make_async_copy(out.at[0], out.at[0], recv2.at[size + i]).wait()
    return result


def exchange_end(tracks, sessions, src, middle, send, send2):
    sent = src.at[pl.ds(0, sessions // 2), pl.ds(0, tracks - 1)]
    for h in range(2):
        pltpu.make_async_copy(sent, sent, send.at[h]).wait()
    for i in range(1, sessions):
        pltpu.make_async_copy(middle.at[0], middle.at[0], send2.at[i]).wait()


def reduce_all(me, ses, tracks, sessions, row, out, mine, middle, partial, final, send, recv, send2, recv2, local):
    mine[...] = row

    def track(i, _):
        to = lax.rem(me + i, tracks)
        pltpu.make_async_remote_copy(
            mine, middle.at[me], send, recv, device_id={"track": to}, device_id_type=MESH
        ).start()
        return 0

    lax.fori_loop(1, tracks, track, 0)
    own = pltpu.make_async_copy(mine, middle.at[me], local.at[0])
    own.start()
    own.wait()
    others = pl.ds(0, tracks - 1)
    pltpu.make_async_copy(middle.at[others], middle.at[others], recv).wait()
    partial[...] = jnp.sum(middle[...], axis=0)
    for i in range(1, sessions):
        to = lax.rem(ses + i, sessions)
        pltpu.make_async_remote_copy(
            partial, final.at[ses], send2.at[i], recv2.at[i], device_id={"ses": to}, device_id_type=MESH
        ).start()
    own = pltpu.make_async_copy(partial, final.at[ses], local.at[1])
    own.start()
    own.wait()
    for i in range(1, sessions):
        block = final.at[lax.rem(ses - i + sessions, sessions)]
        pltpu.make_async_copy(block, block, recv2.at[i]).wait()
        pltpu.make_async_copy(partial, partial, send2.at[i]).wait()
    out[...] = jnp.sum(final[...], axis=0)
    pltpu.make_async_copy(middle.at[others], middle.at[others], send).wait()


def step_kernel(
    tracks, sessions,
    direction_ref, rows_ref, slot_ref, mask_ref, land_ref, jac_hbm, residual_hbm, damp_hbm, precond_hbm,
    schur_ref, pre_res_ref, pre_schur_ref, sums_ref,
    jac_ref, residual_ref, damp_ref, precond_ref, loads,
    index, tiles, swap, hot, owner_hot, src1, middle1, out1, src2, middle2, out2, row, middle3, partial, final,
    sems1, sems2, sems3,
):
    me, ses, barrier = greet(tracks, sessions)
    pairs = ((residual_hbm, residual_ref), (precond_hbm, precond_ref), (jac_hbm, jac_ref), (damp_hbm, damp_ref))
    copies = [pltpu.make_async_copy(src, dst, loads.at[i]) for i, (src, dst) in enumerate(pairs)]
    for copy in copies:
        copy.start()
    capacity = index.shape[0]
    turn_rows(rows_ref, tracks, sessions, capacity, index)
    serve(direction_ref, index, hot, src1, tiles)
    pl.semaphore_wait(barrier, tracks + sessions - 2)

    def during_first():
        for copy in copies:
            copy.wait()
        owner_hots(slot_ref, sessions, tracks, capacity, owner_hot)
        return residual_terms(residual_ref, precond_ref, pre_res_ref)

    old = exchange(me, ses, tracks, sessions, src1, middle1, out1, *sems1, during_first)
    track_terms(out1, jac_ref, land_ref, slot_ref, mask_ref, owner_hot, src2, swap)
    exchange(
        me, ses, tracks, sessions, src2, middle2, out2, *sems2,
        lambda: exchange_end(tracks, sessions, src1, middle1, sems1[0], sems1[2]),
    )
    rest = schur_terms(
        out2, index, hot, direction_ref, damp_ref, precond_ref, pre_res_ref, schur_ref, pre_schur_ref, tiles
    )
    reduce_all(
        me, ses, tracks, sessions, sums_row([old] + rest), sums_ref, row, middle3, partial, final, *sems3
    )
    exchange_end(tracks, sessions, src2, middle2, sems2[0], sems2[2])


def local_call(kernel, outs, scratch, *args):
    return pl.pallas_call(
        kernel,
        out_shape=[jax.ShapeDtypeStruct(s, jnp.float32) for s in outs],
        in_specs=[VMEM] * len(args),
        out_specs=[VMEM] * len(outs),
        scratch_shapes=[pltpu.VMEM(s, jnp.float32) for s in scratch],
        name=kernel.__name__,
    )(*args)


def on_device(
    jacobians, direction, residual, solution, cam_damping, precond, land_damping, obs_slot, obs_mask, serve_rows
):
    tracks, sessions = lax.axis_size("track"), lax.axis_size("ses")
    devices = tracks * sessions
    capacity = serve_rows.size // devices
    width = capacity * KEYS
    slots, observed = obs_slot.shape
    shape = direction.shape
    dma = pltpu.SemaphoreType.DMA
    block = pltpu.VMEM((sessions, tracks, width), jnp.float32)
    line = (1, 128)
    sems = [dma((2,)), dma((2,)), dma((sessions,)), dma((sessions,)), dma((2,))]
    small = (direction, serve_rows, obs_slot, obs_mask, land_damping[None])
    large = (jacobians, residual, cam_damping, precond)
    schur, pre_res, pre_schur, sums = pl.pallas_call(
        functools.partial(step_kernel, tracks, sessions),
        out_shape=[jax.ShapeDtypeStruct(s, jnp.float32) for s in (shape, shape, shape, line)],
        in_specs=[VMEM] * len(small) + [pl.BlockSpec(memory_space=pl.ANY)] * len(large),
        out_specs=[VMEM] * 4,
        scratch_shapes=[pltpu.VMEM(x.shape, x.dtype) for x in large]
        + [
            dma((len(large),)),
            pltpu.VMEM((capacity, devices), jnp.int32),
            pltpu.VMEM((devices // 128, capacity * SLOT, 128), jnp.float32),
            pltpu.VMEM((slots * KEYS, observed), jnp.float32),
            pltpu.VMEM((capacity, LANES, devices), jnp.bfloat16),
            pltpu.VMEM((slots, devices, observed), jnp.bfloat16),
        ]
        + [block] * 6
        + [
            pltpu.VMEM(line, jnp.float32),
            pltpu.VMEM((tracks,) + line, jnp.float32),
            pltpu.VMEM(line, jnp.float32),
            pltpu.VMEM((sessions,) + line, jnp.float32),
            tuple(sems),
            tuple(sems),
            (dma, dma, dma((sessions,)), dma((sessions,)), dma((2,))),
        ],
        compiler_params=pltpu.CompilerParams(collective_id=0, has_side_effects=True),
        name="step",
    )(*small, *large)
    return tuple(
        local_call(update_kernel, [shape] * 3, [], sums, direction, residual, solution, schur, pre_res, pre_schur)
    )


def solution(mesh):
    split = ("track", "ses")
    return jax.shard_map(
        on_device,
        mesh=mesh,
        in_specs=(
            P(None, None, None, split),
            P(None, split),
            P(None, split),
            P(None, split),
            P(None, split),
            P(None, None, split),
            P(split),
            P(None, split),
            P(None, split),
            P(split, None),
        ),
        out_specs=(P(None, split), P(None, split), P(None, split)),
        check_vma=False,
    )
```

```python
import functools

import jax
import jax.numpy as jnp
from jax import lax
from jax.experimental import pallas as pl
from jax.experimental.pallas import tpu as pltpu
from jax.sharding import PartitionSpec as P

MESH = pl.DeviceIdType.MESH
VMEM = pl.BlockSpec(memory_space=pltpu.VMEM)
LANES = 256
KEYS = 6
SLOT = 8


def pieces(x):
    high = x.astype(jnp.bfloat16)
    low = (x - high.astype(jnp.float32)).astype(jnp.bfloat16)
    return jnp.concatenate([high, low], axis=0)


def join(x):
    half = x.shape[0] // 2
    return x[:half] + x[half:]


def one_hot(index, size):
    rows = lax.broadcasted_iota(jnp.int32, (size, index.shape[1]), 0)
    return jnp.where(rows == index, 1.0, 0.0).astype(jnp.bfloat16)


def pick(values, group):
    total = jnp.zeros((SLOT, values.shape[1]), jnp.float32)
    for g in range(values.shape[0] // SLOT):
        total += jnp.where(group == g, values[g * SLOT : (g + 1) * SLOT], 0.0)
    return total


def spread(values, group, groups):
    return jnp.concatenate([jnp.where(group == g, values, 0.0) for g in range(groups)], axis=0)


def slot_mask(within, capacity):
    return lax.broadcasted_iota(jnp.int32, (capacity, within.shape[1]), 0) == within


def dot(a, b):
    return lax.dot_general(a, b, (((1,), (0,)), ((), ())), preferred_element_type=jnp.float32)


def dot_nt(a, b):
    return lax.dot_general(a, b, (((1,), (1,)), ((), ())), preferred_element_type=jnp.float32)


def turn_rows(rows_ref, tracks, sessions, capacity, index):
    width = sessions * capacity
    turned = jnp.concatenate([rows_ref[:, t * width : (t + 1) * width] for t in range(tracks)], axis=0).T
    for w in range(capacity):
        lines = [turned[y * capacity + w : y * capacity + w + 1, :] for y in range(sessions)]
        index[w : w + 1, :] = jnp.concatenate(lines, axis=1)


def serve(direction_ref, index_ref, hot_ref, out_ref, tiles):
    groups = direction_ref.shape[1] // LANES
    capacity = index_ref.shape[0]
    pad = jnp.zeros((2, LANES), jnp.float32)
    table = []
    for g in range(groups):
        table += [direction_ref[:, g * LANES : (g + 1) * LANES], pad]
    table = pieces(jnp.concatenate(table, axis=0))
    for w in range(capacity):
        index = index_ref[w : w + 1, :]
        hot = one_hot(index & (LANES - 1), LANES)
        hot_ref[w] = hot
        found = pick(join(dot(table, hot)), index // LANES)
        for j in range(tiles.shape[0]):
            tiles[j, pl.ds(w, SLOT, stride=capacity), :] = found[:, j * 128 : (j + 1) * 128]
    turned = [tiles[j, : KEYS * capacity, :].T for j in range(tiles.shape[0])]
    out_ref[...] = jnp.concatenate(turned, axis=0).reshape(out_ref.shape)


def inverse_times(m, rhs):
    a, b, c, d, e, f = m
    c00 = d * f - e * e
    c01 = e * c - b * f
    c02 = b * e - d * c
    c11 = f * a - c * c
    c12 = c * b - e * a
    c22 = a * d - b * b
    scale = 1.0 / (a * c00 + b * c01 + c * c02)
    x, y, z = rhs
    return (
        (c00 * x + c01 * y + c02 * z) * scale,
        (c01 * x + c11 * y + c12 * z) * scale,
        (c02 * x + c12 * y + c22 * z) * scale,
    )


def owner_hots(slot_ref, sessions, tracks, capacity, hot_ref):
    for o in range(slot_ref.shape[0]):
        owner = slot_ref[o : o + 1, :] // capacity
        place = lax.rem(owner, sessions) * tracks + owner // sessions
        hot_ref[o] = one_hot(place, sessions * tracks)


def track_terms(incoming_ref, jac_ref, damp_ref, slot_ref, mask_ref, hot_ref, out_ref, swap):
    sessions, track_count, width = incoming_ref.shape
    devices = sessions * track_count
    capacity = width // KEYS
    slots = slot_ref.shape[0]
    table = pieces(incoming_ref[...].reshape(devices, width).T)
    masks = [slot_mask(slot_ref[o : o + 1, :] % capacity, capacity) for o in range(slots)]
    for o in range(slots):
        found = join(dot(table, hot_ref[o]))
        for k in range(KEYS):
            chosen = jnp.where(masks[o], found[k * capacity : (k + 1) * capacity], 0.0)
            swap[k * slots + o : k * slots + o + 1, :] = jnp.sum(chosen, axis=0, keepdims=True)
    camera = [swap[k * slots : (k + 1) * slots, :] for k in range(KEYS)]
    live = mask_ref[...].astype(jnp.float32)
    cam = [[jac_ref[a, k] for k in range(6)] for a in range(2)]
    land = [[jac_ref[a, 6 + i] for i in range(3)] for a in range(2)]
    projected = [sum(cam[a][k] * camera[k] for k in range(6)) for a in range(2)]
    weighted = [[land[a][i] * live for i in range(3)] for a in range(2)]

    def over(x):
        return jnp.sum(x, axis=0, keepdims=True)

    damp = damp_ref[...]
    normal = []
    for i in range(3):
        for j in range(i, 3):
            entry = over(sum(weighted[a][i] * land[a][j] for a in range(2)))
            normal.append(entry + damp if i == j else entry)
    rhs = [over(sum(weighted[a][i] * projected[a] for a in range(2))) for i in range(3)]
    step = inverse_times(normal, rhs)
    res = [live * (projected[a] - sum(land[a][i] * step[i] for i in range(3))) for a in range(2)]
    gradient = [sum(cam[a][k] * res[a] for a in range(2)) for k in range(6)]
    total = jnp.zeros((2 * width, devices), jnp.float32)
    for o in range(slots):
        terms = [jnp.where(masks[o], gradient[k][o : o + 1], 0.0) for k in range(KEYS)]
        total += dot_nt(pieces(jnp.concatenate(terms, axis=0)), hot_ref[o])
    out_ref[...] = join(total).T.reshape(out_ref.shape)


def apply_precond(precond, vector):
    total = precond[0] * vector[0:1]
    for k in range(1, 6):
        total += precond[k] * vector[k : k + 1]
    return total


def residual_terms(residual_ref, precond_ref, pre_res_ref):
    total = jnp.zeros((6, LANES), jnp.float32)
    for g in range(residual_ref.shape[1] // LANES):
        part = pl.ds(g * LANES, LANES)
        residual = residual_ref[:, part]
        pre_res = apply_precond(precond_ref[:, :, part], residual)
        pre_res_ref[:, part] = pre_res
        total += residual * pre_res
    return total


def schur_terms(
    arrived_ref, index_ref, hot_ref, direction_ref, damp_ref, precond_ref, pre_res_ref, schur_ref, pre_schur_ref, tiles
):
    groups = direction_ref.shape[1] // LANES
    sessions, tracks, width = arrived_ref.shape
    capacity = index_ref.shape[0]
    turned = arrived_ref[...].reshape(sessions * tracks, width).T
    count = tiles.shape[0]
    for j in range(count):
        tiles[j, :width, :] = turned[:, j * 128 : (j + 1) * 128]
    total = jnp.zeros((2 * groups * SLOT, LANES), jnp.float32)
    for w in range(index_ref.shape[0]):
        index = index_ref[w : w + 1, :]
        lines = [tiles[j, pl.ds(w, SLOT, stride=capacity), :] for j in range(count)]
        terms = pieces(spread(jnp.concatenate(lines, axis=1), index // LANES, groups))
        total += dot_nt(terms, hot_ref[w])
    total = join(total)
    sums = [jnp.zeros((6, LANES), jnp.float32) for _ in range(3)]
    for g in range(groups):
        part = pl.ds(g * LANES, LANES)
        direction = direction_ref[:, part]
        schur = damp_ref[:, part] * direction + total[g * SLOT : g * SLOT + 6]
        pre_schur = apply_precond(precond_ref[:, :, part], schur)
        schur_ref[:, part] = schur
        pre_schur_ref[:, part] = pre_schur
        sums[0] += direction * schur
        sums[1] += schur * pre_res_ref[:, part]
        sums[2] += schur * pre_schur
    return sums


def sums_row(sums):
    lane = lax.broadcasted_iota(jnp.int32, (1, 128), 1)
    row = jnp.zeros((1, 128), jnp.float32)
    for q in range(4):
        row += jnp.where(lane == q, jnp.sum(sums[q], keepdims=True), 0.0)
    return row


def update_kernel(
    sums_ref, direction_ref, residual_ref, solution_ref, schur_ref, pre_res_ref, pre_schur_ref,
    solution_new_ref, residual_new_ref, direction_new_ref,
):
    old_norm, curvature, cross, square = [sums_ref[0:1, q : q + 1] for q in range(4)]
    step = old_norm / curvature
    ratio = (old_norm - 2.0 * step * cross + step * step * square) / old_norm
    direction = direction_ref[...]
    solution_new_ref[...] = solution_ref[...] + step * direction
    residual_new_ref[...] = residual_ref[...] - step * schur_ref[...]
    direction_new_ref[...] = pre_res_ref[...] - step * pre_schur_ref[...] + ratio * direction


def far_first(me, j, tracks):
    step = (j + 1) // 2 * (2 * lax.rem(j, 2) - 1)
    return lax.rem(me + tracks // 2 + step, tracks)


def greet(tracks, sessions):
    me, ses = lax.axis_index("track"), lax.axis_index("ses")
    barrier = pltpu.get_barrier_semaphore()

    def track(i, _):
        pl.semaphore_signal(barrier, inc=1, device_id={"track": far_first(me, i, tracks)}, device_id_type=MESH)
        return 0

    lax.fori_loop(0, tracks - 1, track, 0)
    for i in range(1, sessions):
        pl.semaphore_signal(barrier, inc=1, device_id={"ses": lax.rem(ses + i, sessions)}, device_id_type=MESH)
    return me, ses, barrier


def send_tracks(me, tracks, src, src_at, size, dst, dst_at, send, recv):
    def track(i, _):
        to = far_first(me, i, tracks)
        pltpu.make_async_remote_copy(
            src.at[pl.ds(src_at, size), to], dst.at[pl.ds(dst_at, size), me], send, recv,
            device_id={"track": to}, device_id_type=MESH,
        ).start()
        return 0

    lax.fori_loop(0, tracks - 1, track, 0)


def send_session(ses, to, src, dst, send, recv):
    pltpu.make_async_remote_copy(src, dst, send, recv, device_id={"ses": to}, device_id_type=MESH).start()


def exchange(me, ses, tracks, sessions, src, middle, out, send, recv, send2, recv2, local, between):
    size = sessions // 2
    mine = ses // size * size
    other = size - mine
    inner = lax.rem(ses, size)
    for i in range(1, size):
        to = mine + lax.rem(inner + i, size)
        send_session(ses, to, src.at[to], middle.at[ses], send2.at[i], recv2.at[i])
    send_tracks(me, tracks, src, other, size, middle, other, send.at[0], recv.at[0])
    own = [
        pltpu.make_async_copy(src.at[ses], middle.at[ses], local.at[0]),
        pltpu.make_async_copy(src.at[pl.ds(other, size), me], middle.at[pl.ds(other, size), me], local.at[1]),
    ]
    for copy in own:
        copy.start()
    for copy in own:
        copy.wait()
    for i in range(1, size):
        pltpu.make_async_copy(out.at[0], out.at[0], recv2.at[i]).wait()
    send_tracks(me, tracks, middle, mine, size, out, mine, send.at[1], recv.at[1])
    result = between()
    waits = out.at[pl.ds(0, size), pl.ds(0, tracks - 1)]
    pltpu.make_async_copy(waits, waits, recv.at[0]).wait()
    for i in range(size):
        to = other + lax.rem(inner + i, size)
        send_session(ses, to, middle.at[to], out.at[ses], send2.at[size + i], recv2.at[size + i])
    last = pltpu.make_async_copy(middle.at[pl.ds(mine, size), me], out.at[pl.ds(mine, size), me], local.at[0])
    last.start()
    last.wait()
    pltpu.make_async_copy(waits, waits, recv.at[1]).wait()
    for i in range(size):
        pltpu.make_async_copy(out.at[0], out.at[0], recv2.at[size + i]).wait()
    return result


def exchange_end(tracks, sessions, src, middle, send, send2):
    sent = src.at[pl.ds(0, sessions // 2), pl.ds(0, tracks - 1)]
    for h in range(2):
        pltpu.make_async_copy(sent, sent, send.at[h]).wait()
    for i in range(1, sessions):
        pltpu.make_async_copy(middle.at[0], middle.at[0], send2.at[i]).wait()


def reduce_all(me, ses, tracks, sessions, row, out, mine, middle, partial, final, send, recv, send2, recv2, local):
    mine[...] = row

    def track(i, _):
        to = far_first(me, i, tracks)
        pltpu.make_async_remote_copy(
            mine, middle.at[me], send, recv, device_id={"track": to}, device_id_type=MESH
        ).start()
        return 0

    lax.fori_loop(0, tracks - 1, track, 0)
    own = pltpu.make_async_copy(mine, middle.at[me], local.at[0])
    own.start()
    own.wait()
    others = pl.ds(0, tracks - 1)
    pltpu.make_async_copy(middle.at[others], middle.at[others], recv).wait()
    partial[...] = jnp.sum(middle[...], axis=0)
    for i in range(1, sessions):
        to = lax.rem(ses + i, sessions)
        pltpu.make_async_remote_copy(
            partial, final.at[ses], send2.at[i], recv2.at[i], device_id={"ses": to}, device_id_type=MESH
        ).start()
    own = pltpu.make_async_copy(partial, final.at[ses], local.at[1])
    own.start()
    own.wait()
    for i in range(1, sessions):
        block = final.at[lax.rem(ses - i + sessions, sessions)]
        pltpu.make_async_copy(block, block, recv2.at[i]).wait()
        pltpu.make_async_copy(partial, partial, send2.at[i]).wait()
    out[...] = jnp.sum(final[...], axis=0)
    pltpu.make_async_copy(middle.at[others], middle.at[others], send).wait()


def step_kernel(
    tracks, sessions,
    direction_ref, rows_ref, slot_ref, mask_ref, land_ref, jac_hbm, residual_hbm, damp_hbm, precond_hbm,
    schur_ref, pre_res_ref, pre_schur_ref, sums_ref,
    jac_ref, residual_ref, damp_ref, precond_ref, loads,
    index, tiles, swap, hot, owner_hot, src1, middle1, out1, src2, middle2, out2, row, middle3, partial, final,
    sems1, sems2, sems3,
):
    me, ses, barrier = greet(tracks, sessions)
    pairs = ((residual_hbm, residual_ref), (precond_hbm, precond_ref), (jac_hbm, jac_ref), (damp_hbm, damp_ref))
    copies = [pltpu.make_async_copy(src, dst, loads.at[i]) for i, (src, dst) in enumerate(pairs)]
    for copy in copies:
        copy.start()
    capacity = index.shape[0]
    turn_rows(rows_ref, tracks, sessions, capacity, index)
    serve(direction_ref, index, hot, src1, tiles)
    pl.semaphore_wait(barrier, tracks + sessions - 2)

    def during_first():
        for copy in copies:
            copy.wait()
        owner_hots(slot_ref, sessions, tracks, capacity, owner_hot)
        return residual_terms(residual_ref, precond_ref, pre_res_ref)

    old = exchange(me, ses, tracks, sessions, src1, middle1, out1, *sems1, during_first)
    track_terms(out1, jac_ref, land_ref, slot_ref, mask_ref, owner_hot, src2, swap)
    exchange(
        me, ses, tracks, sessions, src2, middle2, out2, *sems2,
        lambda: exchange_end(tracks, sessions, src1, middle1, sems1[0], sems1[2]),
    )
    rest = schur_terms(
        out2, index, hot, direction_ref, damp_ref, precond_ref, pre_res_ref, schur_ref, pre_schur_ref, tiles
    )
    reduce_all(
        me, ses, tracks, sessions, sums_row([old] + rest), sums_ref, row, middle3, partial, final, *sems3
    )
    exchange_end(tracks, sessions, src2, middle2, sems2[0], sems2[2])


def local_call(kernel, outs, scratch, *args):
    return pl.pallas_call(
        kernel,
        out_shape=[jax.ShapeDtypeStruct(s, jnp.float32) for s in outs],
        in_specs=[VMEM] * len(args),
        out_specs=[VMEM] * len(outs),
        scratch_shapes=[pltpu.VMEM(s, jnp.float32) for s in scratch],
        name=kernel.__name__,
    )(*args)


def on_device(
    jacobians, direction, residual, solution, cam_damping, precond, land_damping, obs_slot, obs_mask, serve_rows
):
    tracks, sessions = lax.axis_size("track"), lax.axis_size("ses")
    devices = tracks * sessions
    capacity = serve_rows.size // devices
    width = capacity * KEYS
    slots, observed = obs_slot.shape
    shape = direction.shape
    dma = pltpu.SemaphoreType.DMA
    block = pltpu.VMEM((sessions, tracks, width), jnp.float32)
    line = (1, 128)
    sems = [dma((2,)), dma((2,)), dma((sessions,)), dma((sessions,)), dma((2,))]
    small = (direction, serve_rows, obs_slot, obs_mask, land_damping[None])
    large = (jacobians, residual, cam_damping, precond)
    schur, pre_res, pre_schur, sums = pl.pallas_call(
        functools.partial(step_kernel, tracks, sessions),
        out_shape=[jax.ShapeDtypeStruct(s, jnp.float32) for s in (shape, shape, shape, line)],
        in_specs=[VMEM] * len(small) + [pl.BlockSpec(memory_space=pl.ANY)] * len(large),
        out_specs=[VMEM] * 4,
        scratch_shapes=[pltpu.VMEM(x.shape, x.dtype) for x in large]
        + [
            dma((len(large),)),
            pltpu.VMEM((capacity, devices), jnp.int32),
            pltpu.VMEM((devices // 128, capacity * SLOT, 128), jnp.float32),
            pltpu.VMEM((slots * KEYS, observed), jnp.float32),
            pltpu.VMEM((capacity, LANES, devices), jnp.bfloat16),
            pltpu.VMEM((slots, devices, observed), jnp.bfloat16),
        ]
        + [block] * 6
        + [
            pltpu.VMEM(line, jnp.float32),
            pltpu.VMEM((tracks,) + line, jnp.float32),
            pltpu.VMEM(line, jnp.float32),
            pltpu.VMEM((sessions,) + line, jnp.float32),
            tuple(sems),
            tuple(sems),
            (dma, dma, dma((sessions,)), dma((sessions,)), dma((2,))),
        ],
        compiler_params=pltpu.CompilerParams(collective_id=0, has_side_effects=True),
        name="step",
    )(*small, *large)
    return tuple(
        local_call(update_kernel, [shape] * 3, [], sums, direction, residual, solution, schur, pre_res, pre_schur)
    )


def solution(mesh):
    split = ("track", "ses")
    return jax.shard_map(
        on_device,
        mesh=mesh,
        in_specs=(
            P(None, None, None, split),
            P(None, split),
            P(None, split),
            P(None, split),
            P(None, split),
            P(None, None, split),
            P(split),
            P(None, split),
            P(None, split),
            P(split, None),
        ),
        out_specs=(P(None, split), P(None, split), P(None, split)),
        check_vma=False,
    )
```

```python
import functools

import jax
import jax.numpy as jnp
from jax import lax
from jax.experimental import pallas as pl
from jax.experimental.pallas import tpu as pltpu
from jax.sharding import PartitionSpec as P

MESH = pl.DeviceIdType.MESH
VMEM = pl.BlockSpec(memory_space=pltpu.VMEM)
LANES = 256
KEYS = 6
SLOT = 8


def pieces(x):
    high = x.astype(jnp.bfloat16)
    low = (x - high.astype(jnp.float32)).astype(jnp.bfloat16)
    return jnp.concatenate([high, low], axis=0)


def join(x):
    half = x.shape[0] // 2
    return x[:half] + x[half:]


def one_hot(index, size):
    rows = lax.broadcasted_iota(jnp.int32, (size, index.shape[1]), 0)
    return jnp.where(rows == index, 1.0, 0.0).astype(jnp.bfloat16)


def pick(values, group):
    total = jnp.zeros((SLOT, values.shape[1]), jnp.float32)
    for g in range(values.shape[0] // SLOT):
        total += jnp.where(group == g, values[g * SLOT : (g + 1) * SLOT], 0.0)
    return total


def spread(values, group, groups):
    return jnp.concatenate([jnp.where(group == g, values, 0.0) for g in range(groups)], axis=0)


def slot_mask(within, capacity):
    return lax.broadcasted_iota(jnp.int32, (capacity, within.shape[1]), 0) == within


def dot(a, b):
    return lax.dot_general(a, b, (((1,), (0,)), ((), ())), preferred_element_type=jnp.float32)


def dot_nt(a, b):
    return lax.dot_general(a, b, (((1,), (1,)), ((), ())), preferred_element_type=jnp.float32)


def turn_rows(rows_ref, tracks, sessions, capacity, index):
    width = sessions * capacity
    turned = jnp.concatenate([rows_ref[:, t * width : (t + 1) * width] for t in range(tracks)], axis=0).T
    for w in range(capacity):
        lines = [turned[y * capacity + w : y * capacity + w + 1, :] for y in range(sessions)]
        index[w : w + 1, :] = jnp.concatenate(lines, axis=1)


def serve(direction_ref, index_ref, hot_ref, out_ref, tiles):
    groups = direction_ref.shape[1] // LANES
    capacity = index_ref.shape[0]
    pad = jnp.zeros((2, LANES), jnp.float32)
    table = []
    for g in range(groups):
        table += [direction_ref[:, g * LANES : (g + 1) * LANES], pad]
    table = pieces(jnp.concatenate(table, axis=0))
    for w in range(capacity):
        index = index_ref[w : w + 1, :]
        hot = one_hot(index & (LANES - 1), LANES)
        hot_ref[w] = hot
        found = pick(join(dot(table, hot)), index // LANES)
        for j in range(tiles.shape[0]):
            tiles[j, pl.ds(w, SLOT, stride=capacity), :] = found[:, j * 128 : (j + 1) * 128]
    turned = [tiles[j, : KEYS * capacity, :].T for j in range(tiles.shape[0])]
    out_ref[...] = jnp.concatenate(turned, axis=0).reshape(out_ref.shape)


def inverse_times(m, rhs):
    a, b, c, d, e, f = m
    c00 = d * f - e * e
    c01 = e * c - b * f
    c02 = b * e - d * c
    c11 = f * a - c * c
    c12 = c * b - e * a
    c22 = a * d - b * b
    scale = 1.0 / (a * c00 + b * c01 + c * c02)
    x, y, z = rhs
    return (
        (c00 * x + c01 * y + c02 * z) * scale,
        (c01 * x + c11 * y + c12 * z) * scale,
        (c02 * x + c12 * y + c22 * z) * scale,
    )


def owner_hots(slot_ref, sessions, tracks, capacity, hot_ref):
    for o in range(slot_ref.shape[0]):
        owner = slot_ref[o : o + 1, :] // capacity
        place = lax.rem(owner, sessions) * tracks + owner // sessions
        hot_ref[o] = one_hot(place, sessions * tracks)


def track_terms(incoming_ref, jac_ref, damp_ref, slot_ref, mask_ref, hot_ref, out_ref, swap):
    sessions, track_count, width = incoming_ref.shape
    devices = sessions * track_count
    capacity = width // KEYS
    slots = slot_ref.shape[0]
    table = pieces(incoming_ref[...].reshape(devices, width).T)
    masks = [slot_mask(slot_ref[o : o + 1, :] % capacity, capacity) for o in range(slots)]
    for o in range(slots):
        found = join(dot(table, hot_ref[o]))
        for k in range(KEYS):
            chosen = jnp.where(masks[o], found[k * capacity : (k + 1) * capacity], 0.0)
            swap[k * slots + o : k * slots + o + 1, :] = jnp.sum(chosen, axis=0, keepdims=True)
    camera = [swap[k * slots : (k + 1) * slots, :] for k in range(KEYS)]
    live = mask_ref[...].astype(jnp.float32)
    cam = [[jac_ref[a, k] for k in range(6)] for a in range(2)]
    land = [[jac_ref[a, 6 + i] for i in range(3)] for a in range(2)]
    projected = [sum(cam[a][k] * camera[k] for k in range(6)) for a in range(2)]
    weighted = [[land[a][i] * live for i in range(3)] for a in range(2)]

    def over(x):
        return jnp.sum(x, axis=0, keepdims=True)

    damp = damp_ref[...]
    normal = []
    for i in range(3):
        for j in range(i, 3):
            entry = over(sum(weighted[a][i] * land[a][j] for a in range(2)))
            normal.append(entry + damp if i == j else entry)
    rhs = [over(sum(weighted[a][i] * projected[a] for a in range(2))) for i in range(3)]
    step = inverse_times(normal, rhs)
    res = [live * (projected[a] - sum(land[a][i] * step[i] for i in range(3))) for a in range(2)]
    gradient = [sum(cam[a][k] * res[a] for a in range(2)) for k in range(6)]
    total = jnp.zeros((2 * width, devices), jnp.float32)
    for o in range(slots):
        terms = [jnp.where(masks[o], gradient[k][o : o + 1], 0.0) for k in range(KEYS)]
        total += dot_nt(pieces(jnp.concatenate(terms, axis=0)), hot_ref[o])
    out_ref[...] = join(total).T.reshape(out_ref.shape)


def apply_precond(precond, vector):
    total = precond[0] * vector[0:1]
    for k in range(1, 6):
        total += precond[k] * vector[k : k + 1]
    return total


def residual_terms(residual_ref, precond_ref, pre_res_ref):
    total = jnp.zeros((6, LANES), jnp.float32)
    for g in range(residual_ref.shape[1] // LANES):
        part = pl.ds(g * LANES, LANES)
        residual = residual_ref[:, part]
        pre_res = apply_precond(precond_ref[:, :, part], residual)
        pre_res_ref[:, part] = pre_res
        total += residual * pre_res
    return total


def schur_terms(
    arrived_ref, index_ref, hot_ref, direction_ref, damp_ref, precond_ref, pre_res_ref, schur_ref, pre_schur_ref, tiles
):
    groups = direction_ref.shape[1] // LANES
    sessions, tracks, width = arrived_ref.shape
    capacity = index_ref.shape[0]
    turned = arrived_ref[...].reshape(sessions * tracks, width).T
    count = tiles.shape[0]
    for j in range(count):
        tiles[j, :width, :] = turned[:, j * 128 : (j + 1) * 128]
    total = jnp.zeros((2 * groups * SLOT, LANES), jnp.float32)
    for w in range(index_ref.shape[0]):
        index = index_ref[w : w + 1, :]
        lines = [tiles[j, pl.ds(w, SLOT, stride=capacity), :] for j in range(count)]
        terms = pieces(spread(jnp.concatenate(lines, axis=1), index // LANES, groups))
        total += dot_nt(terms, hot_ref[w])
    total = join(total)
    sums = [jnp.zeros((6, LANES), jnp.float32) for _ in range(3)]
    for g in range(groups):
        part = pl.ds(g * LANES, LANES)
        direction = direction_ref[:, part]
        schur = damp_ref[:, part] * direction + total[g * SLOT : g * SLOT + 6]
        pre_schur = apply_precond(precond_ref[:, :, part], schur)
        schur_ref[:, part] = schur
        pre_schur_ref[:, part] = pre_schur
        sums[0] += direction * schur
        sums[1] += schur * pre_res_ref[:, part]
        sums[2] += schur * pre_schur
    return sums


def sums_row(sums):
    lane = lax.broadcasted_iota(jnp.int32, (1, 128), 1)
    row = jnp.zeros((1, 128), jnp.float32)
    for q in range(4):
        row += jnp.where(lane == q, jnp.sum(sums[q], keepdims=True), 0.0)
    return row


def update_kernel(
    sums_ref, direction_ref, residual_ref, solution_ref, schur_ref, pre_res_ref, pre_schur_ref,
    solution_new_ref, residual_new_ref, direction_new_ref,
):
    old_norm, curvature, cross, square = [sums_ref[0:1, q : q + 1] for q in range(4)]
    step = old_norm / curvature
    ratio = (old_norm - 2.0 * step * cross + step * step * square) / old_norm
    direction = direction_ref[...]
    solution_new_ref[...] = solution_ref[...] + step * direction
    residual_new_ref[...] = residual_ref[...] - step * schur_ref[...]
    direction_new_ref[...] = pre_res_ref[...] - step * pre_schur_ref[...] + ratio * direction


def far_first(me, j, tracks):
    step = (j + 1) // 2 * (2 * lax.rem(j, 2) - 1)
    return lax.rem(me + tracks // 2 + step, tracks)


def greet(tracks, sessions):
    me, ses = lax.axis_index("track"), lax.axis_index("ses")
    barrier = pltpu.get_barrier_semaphore()

    def track(i, _):
        pl.semaphore_signal(barrier, inc=1, device_id={"track": far_first(me, i, tracks)}, device_id_type=MESH)
        return 0

    lax.fori_loop(0, tracks - 1, track, 0)
    for i in range(1, sessions):
        pl.semaphore_signal(barrier, inc=1, device_id={"ses": lax.rem(ses + i, sessions)}, device_id_type=MESH)
    return me, ses, barrier


def send_tracks(me, tracks, src, src_at, size, dst, dst_at, send, recv):
    def track(i, _):
        to = far_first(me, i, tracks)
        pltpu.make_async_remote_copy(
            src.at[pl.ds(src_at, size), to], dst.at[pl.ds(dst_at, size), me], send, recv,
            device_id={"track": to}, device_id_type=MESH,
        ).start()
        return 0

    lax.fori_loop(0, tracks - 1, track, 0)


def send_session(ses, to, src, dst, send, recv):
    pltpu.make_async_remote_copy(src, dst, send, recv, device_id={"ses": to}, device_id_type=MESH).start()


def exchange(me, ses, tracks, sessions, src, middle, out, send, recv, send2, recv2, local, between):
    size = sessions // 2
    mine = ses // size * size
    other = size - mine
    inner = lax.rem(ses, size)
    for i in range(1, size):
        to = mine + lax.rem(inner + i, size)
        send_session(ses, to, src.at[to], middle.at[ses], send2.at[i], recv2.at[i])
    send_tracks(me, tracks, src, other, size, middle, other, send.at[0], recv.at[0])
    own = [
        pltpu.make_async_copy(src.at[ses], middle.at[ses], local.at[0]),
        pltpu.make_async_copy(src.at[pl.ds(other, size), me], middle.at[pl.ds(other, size), me], local.at[1]),
    ]
    for copy in own:
        copy.start()
    for copy in own:
        copy.wait()
    for i in range(1, size):
        pltpu.make_async_copy(out.at[0], out.at[0], recv2.at[i]).wait()
    send_tracks(me, tracks, middle, mine, size, out, mine, send.at[1], recv.at[1])
    result = between()
    waits = out.at[pl.ds(0, size), pl.ds(0, tracks - 1)]
    pltpu.make_async_copy(waits, waits, recv.at[0]).wait()
    for i in range(size):
        to = other + lax.rem(inner + i, size)
        send_session(ses, to, middle.at[to], out.at[ses], send2.at[size + i], recv2.at[size + i])
    last = pltpu.make_async_copy(middle.at[pl.ds(mine, size), me], out.at[pl.ds(mine, size), me], local.at[0])
    last.start()
    last.wait()
    pltpu.make_async_copy(waits, waits, recv.at[1]).wait()
    for i in range(size):
        pltpu.make_async_copy(out.at[0], out.at[0], recv2.at[size + i]).wait()
    return result


def exchange_end(tracks, sessions, src, middle, send, send2):
    sent = src.at[pl.ds(0, sessions // 2), pl.ds(0, tracks - 1)]
    for h in range(2):
        pltpu.make_async_copy(sent, sent, send.at[h]).wait()
    for i in range(1, sessions):
        pltpu.make_async_copy(middle.at[0], middle.at[0], send2.at[i]).wait()


def reduce_all(me, ses, tracks, sessions, row, out, mine, middle, partial, final, send, recv, send2, recv2, local):
    mine[...] = row

    def track(i, _):
        to = far_first(me, i, tracks)
        pltpu.make_async_remote_copy(
            mine, middle.at[me], send, recv, device_id={"track": to}, device_id_type=MESH
        ).start()
        return 0

    lax.fori_loop(0, tracks - 1, track, 0)
    own = pltpu.make_async_copy(mine, middle.at[me], local.at[0])
    own.start()
    own.wait()
    others = pl.ds(0, tracks - 1)
    pltpu.make_async_copy(middle.at[others], middle.at[others], recv).wait()
    partial[...] = jnp.sum(middle[...], axis=0)
    for i in range(1, sessions):
        to = lax.rem(ses + i, sessions)
        pltpu.make_async_remote_copy(
            partial, final.at[ses], send2.at[i], recv2.at[i], device_id={"ses": to}, device_id_type=MESH
        ).start()
    own = pltpu.make_async_copy(partial, final.at[ses], local.at[1])
    own.start()
    own.wait()
    for i in range(1, sessions):
        block = final.at[lax.rem(ses - i + sessions, sessions)]
        pltpu.make_async_copy(block, block, recv2.at[i]).wait()
        pltpu.make_async_copy(partial, partial, send2.at[i]).wait()
    out[...] = jnp.sum(final[...], axis=0)
    pltpu.make_async_copy(middle.at[others], middle.at[others], send).wait()


def step_kernel(
    tracks, sessions,
    rows_hbm, direction_hbm, slot_hbm, mask_hbm, land_hbm, residual_hbm, precond_hbm, jac_hbm, damp_hbm,
    schur_ref, pre_res_ref, pre_schur_ref, sums_ref,
    rows_ref, direction_ref, slot_ref, mask_ref, land_ref, residual_ref, precond_ref, jac_ref, damp_ref, loads,
    index, tiles, swap, hot, owner_hot, src1, middle1, out1, src2, middle2, out2, row, middle3, partial, final,
    sems1, sems2, sems3,
):
    sources = (rows_hbm, direction_hbm, slot_hbm, mask_hbm, land_hbm, residual_hbm, precond_hbm, jac_hbm, damp_hbm)
    places = (rows_ref, direction_ref, slot_ref, mask_ref, land_ref, residual_ref, precond_ref, jac_ref, damp_ref)
    copies = [pltpu.make_async_copy(a, b, loads.at[i]) for i, (a, b) in enumerate(zip(sources, places))]
    for copy in copies[:2]:
        copy.start()
    me, ses, barrier = greet(tracks, sessions)
    for copy in copies[2:]:
        copy.start()
    for copy in copies[:2]:
        copy.wait()
    capacity = index.shape[0]
    turn_rows(rows_ref, tracks, sessions, capacity, index)
    serve(direction_ref, index, hot, src1, tiles)
    pl.semaphore_wait(barrier, tracks + sessions - 2)

    def during_first():
        for copy in copies[2:]:
            copy.wait()
        owner_hots(slot_ref, sessions, tracks, capacity, owner_hot)
        return residual_terms(residual_ref, precond_ref, pre_res_ref)

    old = exchange(me, ses, tracks, sessions, src1, middle1, out1, *sems1, during_first)
    track_terms(out1, jac_ref, land_ref, slot_ref, mask_ref, owner_hot, src2, swap)
    exchange(
        me, ses, tracks, sessions, src2, middle2, out2, *sems2,
        lambda: exchange_end(tracks, sessions, src1, middle1, sems1[0], sems1[2]),
    )
    rest = schur_terms(
        out2, index, hot, direction_ref, damp_ref, precond_ref, pre_res_ref, schur_ref, pre_schur_ref, tiles
    )
    reduce_all(
        me, ses, tracks, sessions, sums_row([old] + rest), sums_ref, row, middle3, partial, final, *sems3
    )
    exchange_end(tracks, sessions, src2, middle2, sems2[0], sems2[2])


def local_call(kernel, outs, scratch, *args):
    return pl.pallas_call(
        kernel,
        out_shape=[jax.ShapeDtypeStruct(s, jnp.float32) for s in outs],
        in_specs=[VMEM] * len(args),
        out_specs=[VMEM] * len(outs),
        scratch_shapes=[pltpu.VMEM(s, jnp.float32) for s in scratch],
        name=kernel.__name__,
    )(*args)


def on_device(
    jacobians, direction, residual, solution, cam_damping, precond, land_damping, obs_slot, obs_mask, serve_rows
):
    tracks, sessions = lax.axis_size("track"), lax.axis_size("ses")
    devices = tracks * sessions
    capacity = serve_rows.size // devices
    width = capacity * KEYS
    slots, observed = obs_slot.shape
    shape = direction.shape
    dma = pltpu.SemaphoreType.DMA
    block = pltpu.VMEM((sessions, tracks, width), jnp.float32)
    line = (1, 128)
    sems = [dma((2,)), dma((2,)), dma((sessions,)), dma((sessions,)), dma((2,))]
    args = (
        serve_rows, direction, obs_slot, obs_mask, land_damping[None], residual, precond, jacobians, cam_damping
    )
    schur, pre_res, pre_schur, sums = pl.pallas_call(
        functools.partial(step_kernel, tracks, sessions),
        out_shape=[jax.ShapeDtypeStruct(s, jnp.float32) for s in (shape, shape, shape, line)],
        in_specs=[pl.BlockSpec(memory_space=pl.ANY)] * len(args),
        out_specs=[VMEM] * 4,
        scratch_shapes=[pltpu.VMEM(x.shape, x.dtype) for x in args]
        + [
            dma((len(args),)),
            pltpu.VMEM((capacity, devices), jnp.int32),
            pltpu.VMEM((devices // 128, capacity * SLOT, 128), jnp.float32),
            pltpu.VMEM((slots * KEYS, observed), jnp.float32),
            pltpu.VMEM((capacity, LANES, devices), jnp.bfloat16),
            pltpu.VMEM((slots, devices, observed), jnp.bfloat16),
        ]
        + [block] * 6
        + [
            pltpu.VMEM(line, jnp.float32),
            pltpu.VMEM((tracks,) + line, jnp.float32),
            pltpu.VMEM(line, jnp.float32),
            pltpu.VMEM((sessions,) + line, jnp.float32),
            tuple(sems),
            tuple(sems),
            (dma, dma, dma((sessions,)), dma((sessions,)), dma((2,))),
        ],
        compiler_params=pltpu.CompilerParams(collective_id=0, has_side_effects=True),
        name="step",
    )(*args)
    return tuple(
        local_call(update_kernel, [shape] * 3, [], sums, direction, residual, solution, schur, pre_res, pre_schur)
    )


def solution(mesh):
    split = ("track", "ses")
    return jax.shard_map(
        on_device,
        mesh=mesh,
        in_specs=(
            P(None, None, None, split),
            P(None, split),
            P(None, split),
            P(None, split),
            P(None, split),
            P(None, None, split),
            P(split),
            P(None, split),
            P(None, split),
            P(split, None),
        ),
        out_specs=(P(None, split), P(None, split), P(None, split)),
        check_vma=False,
    )
```
